256 devices in a mesh: task: 8 (over x_hi, y), mp: 32 (over x_lo, z, core).
Axes of the slice: x: 4 (x_hi: 2, x_lo: 2; x = x_hi * 2 + x_lo), y: 4, z: 8, core: 2. Of those that a mesh axis runs over, the one named last changes fastest.
Arguments:
- hidden: bfloat16 [8, 2048, 8192], P('task', 'mp'), may hold values from -6 to 6
- gain: float32 [8192], replicated, may hold values from 0.25 to 1.75
- tau: bfloat16 [8, 8192, 1024], P('task', 'mp'), may hold values from -0.0625 to 0.0625
- coeff: float32 [8, 8192, 1024], P('task', 'mp'), may hold values from 0.1 to 1
- counts: int32 [8], P('task'), may hold values from 683 to 2048, as said below
- positions: int32 [8, 2048], P('task', 'mp'), may hold values from 0 to 2047
Outputs:
- grad_coeff: float32 [8, 8192, 1024], P('task', 'mp')
- loss: float32 [], replicated
The draws below stay inside these ranges and needn't reach their ends.
Inputs may be any that keep to these rules, and one draw needn't show every extreme that they name: `counts`: counts lie between a third of 2048 and 2048; some task has exactly 2048 in every draw. Rows at or past a task's count are not live.
All inputs are finite; a program needn't handle non-finite values.
Results may differ from the reference program's by a relative error of at most 0.0044.
The reference program's roundings to bfloat16 on the way (of `normed`, `merged` and `back`) count: a program that leaves them out, or rounds other values in their place, can miss the bound.
Values may be sent and summed in bfloat16 or wider, within the bound.
A program may use at most 64 MiB of HBM per device.

```python
import jax
import jax.numpy as jnp
from jax import lax

D = 8192
KV = 1024
HEAD = 128
ROWS = 2048
TASKS = 8


def draw_counts(key, part):
    values = jax.random.randint(key, (TASKS,), ROWS // 3 + 1, ROWS + 1)
    chosen = jax.random.randint(jax.random.fold_in(key, 17), (), 0, TASKS)
    return values.at[chosen].set(ROWS).astype(jnp.int32)


def plant(drawn, stream_key, low, high):
    place = [jax.random.randint(jax.random.fold_in(stream_key, axis), (), 0, length) for axis, length in enumerate(drawn.shape)]
    main_axis = drawn.shape.index(max(drawn.shape))
    beside = place[:main_axis] + [(place[main_axis] + 1) % drawn.shape[main_axis]] + place[main_axis + 1:]
    return drawn.at[tuple(place)].set(low).at[tuple(beside)].set(high)


def levels(key, dims, pieces, smallest, top_value):
    level, own = 1.0, jax.random.fold_in(key, 6)
    for axis_at, shards_of in pieces:
        heights = jnp.exp(jax.random.uniform(jax.random.fold_in(own, axis_at), (shards_of,), jnp.float32, smallest / len(pieces), top_value / len(pieces)))
        level = level * jnp.repeat(heights, dims[axis_at] // shards_of).reshape([-1 if axis == axis_at else 1 for axis in range(len(dims))])
    return level


def gaussian(key, dims, scale, limit, split=(), kind=jnp.bfloat16):
    drawn = scale * jax.random.normal(key, dims, jnp.float32)
    if split:
        drawn = drawn * levels(key, dims, split, -0.22, 0.18)
    return jnp.clip(drawn, -limit, limit).astype(kind)


def setup_inputs(seed: int = 0) -> dict:
    seeds = jax.random.split(jax.random.key(seed), 7)
    hidden = gaussian(seeds[0], (TASKS, ROWS, D), 1.0, 6.0, ((0, 8), (1, 32)))
    gain = jnp.clip(1.0 + 0.15 * jax.random.normal(seeds[1], (D,), jnp.float32), 0.25, 1.75)
    tau = gaussian(seeds[2], (TASKS, D, KV), D ** -0.5, 0.0625, ((0, 8), (1, 32)))
    coeff = jnp.clip(0.1 + 0.9 * jax.random.uniform(seeds[3], (TASKS, D, KV), jnp.float32) ** levels(seeds[3], (TASKS, D, KV), ((0, 8), (1, 32)), -0.2, 0.2), 0.1, 1.0)
    counts = draw_counts(jax.random.fold_in(seeds[6], 71), 0)
    positions = plant(jax.random.randint(seeds[5], (TASKS, ROWS), 0, 2048), jax.random.fold_in(seeds[5], 1), 0, 2047).astype(jnp.int32)
    return dict(hidden=hidden, gain=gain, tau=tau, coeff=coeff, counts=counts, positions=positions)


def rotary_tables(positions):
    index = jnp.arange(HEAD // 2).astype(jnp.float32)
    freq = jnp.exp(-jnp.log(jnp.float32(1000000.0)) * 2.0 * index / HEAD)
    angle = positions.astype(jnp.float32)[:, None] * freq[None, :]
    return (jnp.cos(angle), jnp.sin(angle))

def rotate(values, cosine, sine, sign):
    count = values.shape[0]
    shaped = values.reshape(count, KV // HEAD, 2, HEAD // 2)
    first = shaped[:, :, 0, :]
    second = shaped[:, :, 1, :]
    cosine = cosine[:, None, :]
    sine = sine[:, None, :] * sign
    out_first = first * cosine - second * sine
    out_second = second * cosine + first * sine
    return jnp.stack([out_first, out_second], axis=2).reshape(count, KV)

def reference(hidden, gain, tau, coeff, counts, positions):
    mixed = lax.optimization_barrier(jnp.sum(coeff * tau.astype(jnp.float32), axis=0))
    merged = mixed.astype(jnp.bfloat16)
    wgrad = jnp.zeros((D, KV), jnp.float32)
    loss = jnp.zeros((), jnp.float32)
    for task_id in range(TASKS):
        rows = hidden[task_id].astype(jnp.float32)
        inverse = 1.0 / jnp.sqrt(lax.optimization_barrier(jnp.mean(rows * rows, axis=1, keepdims=True)) + 1e-06)
        normed = (rows * inverse * gain[None, :]).astype(jnp.bfloat16)
        teacher = tau[task_id]
        gap = jnp.dot(normed, merged, preferred_element_type=jnp.float32) - jnp.dot(normed, teacher, preferred_element_type=jnp.float32)
        cosine, sine = rotary_tables(positions[task_id])
        err = rotate(gap, cosine, sine, 1.0)
        live = (jnp.arange(ROWS).astype(jnp.int32) < counts[task_id]).astype(jnp.float32)[:, None]
        scale = 1.0 / (counts[task_id].astype(jnp.float32) * KV)
        loss = loss + jnp.sum(live * err * err) * scale
        back = rotate(2.0 * scale * live * err, cosine, sine, -1.0).astype(jnp.bfloat16)
        wgrad = wgrad + jnp.dot(normed.T, back, preferred_element_type=jnp.float32)
    grad_coeff = D * KV * tau.astype(jnp.float32) * wgrad[None, :, :]
    return (grad_coeff, loss)
```

```python
import functools

import jax
import jax.numpy as jnp
from jax import lax
from jax.experimental import pallas as pl
from jax.experimental.pallas import tpu as pltpu
from jax.sharding import PartitionSpec as P

MESH = pl.DeviceIdType.MESH
BF = jnp.bfloat16
F32 = jnp.float32
HEAD = 128
SIZES = dict(xh=2, y=4, xl=2, z=8, c=2)
GROUP = (dict(c=1), dict(xl=1), dict(xl=1, c=1))
TASKS = tuple((a, b) for a in (1, 0) for b in (2, 1, 3, 0) if (a, b) != (0, 0))
RING = (4, 3, 5, 2, 6, 1, 7)
N_SEM = 128


class Links:
    def __init__(self, here, send, recv):
        self.here, self.send, self.recv, self.used, self.open = here, send, recv, 0, []

    def peer(self, **offsets):
        p = dict(self.here)
        for axis, by in offsets.items():
            p[axis] = lax.rem(p[axis] + (by % SIZES[axis]), SIZES[axis])
        return p

    def device(self, p):
        return (p["xh"] * 4 + p["y"], p["xl"] * 16 + p["z"] * 2 + p["c"])

    def copy(self, src, dst, p):
        i = self.used
        self.used += 1
        made = pltpu.make_async_remote_copy(
            src_ref=src,
            dst_ref=dst,
            send_sem=self.send.at[i],
            recv_sem=self.recv.at[i],
            device_id=self.device(p),
            device_id_type=MESH,
        )
        made.start()
        self.open.append(made)
        return made

    def drain(self):
        for made in self.open:
            made.wait_send()


def nt(a, b):
    return lax.dot_general(a, b, (((1,), (1,)), ((), ())), preferred_element_type=F32)


def kernel(
    counts,
    hidden,
    gain,
    tau,
    coeff,
    pos,
    w_out,
    loss_out,
    ns,
    a_all,
    tau_own,
    tau_t,
    m_own,
    m_recv,
    m_half,
    m_recv2,
    m_piece,
    merged,
    gap,
    rs_send,
    rs_recv,
    back,
    w_acc,
    w_send,
    w_recv,
    w_piece,
    w_all,
    pos_all,
    loss_z,
    loss_g,
    loss_t,
    send_sem,
    recv_sem,
    local_sem,
):
    t, m = lax.axis_index("task"), lax.axis_index("mp")
    me = dict(
        xh=lax.div(t, 4),
        y=lax.rem(t, 4),
        xl=lax.div(m, 16),
        z=lax.rem(lax.div(m, 2), 8),
        c=lax.rem(m, 2),
    )
    net = Links(me, send_sem, recv_sem)
    xl, z, c, y, xh = me["xl"], me["z"], me["c"], me["y"], me["xh"]
    g = xl * 2 + c

    barrier = pltpu.get_barrier_semaphore()
    partners = [dict(z=d) for d in RING] + list(GROUP) + [dict(xh=a, y=b) for a, b in TASKS]
    for offsets in partners:
        pl.semaphore_signal(
            barrier, inc=1, device_id=net.device(net.peer(**offsets)), device_id_type=MESH
        )

    total = jnp.zeros((64, 1), F32)
    for k in range(8):
        x = hidden[:, k * 1024 : (k + 1) * 1024].astype(F32)
        total = total + jnp.sum(x * x, axis=1, keepdims=True)
    inverse = 1.0 / jnp.sqrt(total * (1.0 / 8192.0) + 1e-06)
    for k in range(8):
        for half in range(2):
            at = half * 4096 + k * 512
            x = hidden[:, at : at + 512].astype(F32)
            ns[k, :, half * 512 : (half + 1) * 512] = (
                x * inverse * gain[:, at : at + 512]
            ).astype(BF)

    pl.semaphore_wait(barrier, len(partners))

    from_z = []
    for d in RING:
        p = net.peer(z=d)
        from_z.append(net.copy(ns.at[p["z"]], a_all.at[z, xl, c], p))
    sib, xn = net.peer(c=1), net.peer(xl=1)
    own_slot = a_all.at[z, xl, c]
    keep = pltpu.make_async_copy(ns.at[z], own_slot, local_sem.at[0])
    keep.start()
    to_sib, to_x = [], []
    to_sib.append(net.copy(ns.at[z], own_slot, sib))
    to_x.append(net.copy(ns.at[z], own_slot, xn))

    lanes = lax.broadcasted_iota(jnp.int32, (8, 128), 1)
    pos_all[xl, c] = jnp.where(
        lax.div(lanes, 64) == c, jnp.broadcast_to(pos[...], (8, 128)), 0
    )
    small = []
    for offsets in GROUP:
        small.append(net.copy(pos_all.at[xl, c], pos_all.at[xl, c], net.peer(**offsets)))

    for k in range(8):
        cut = slice(k * 128, (k + 1) * 128)
        tau_f = tau[:, cut].astype(F32)
        mixed_t = (coeff[:, cut] * tau_f).T
        m_own[k // 2, 2 * (k % 2) : 2 * (k % 2) + 2] = mixed_t.reshape(2, 2, 32, 256)
        tau_own[k // 2, (k % 2) * 128 : (k % 2) * 128 + 128] = tau_f.T.astype(BF)

    from_y = []
    for i, d in enumerate((2, 1, 3)):
        p = net.peer(y=d)
        from_y.append(net.copy(m_own.at[:, p["y"]], m_recv.at[i], p))
    features = pl.ds(pl.multiple_of(g * 256, 256), 256)
    from_tau = []
    for offsets in GROUP:
        p = net.peer(**offsets)
        from_tau.append(net.copy(tau_own.at[p["xl"] * 2 + p["c"]], tau_t.at[:, features], p))
    keep_tau = pltpu.make_async_copy(tau_own.at[g], tau_t.at[:, features], local_sem.at[1])
    keep_tau.start()

    def forward(i):
        from_z[i].wait_recv()
        slot = a_all.at[lax.rem(z + (8 - RING[i]), 8), xl, c]
        to_sib.append(net.copy(slot, slot, sib))
        to_x.append(net.copy(slot, slot, xn))

    def pass_on(i):
        to_x[i].wait_recv()
        origin = z if i == 0 else lax.rem(z + (8 - RING[i - 1]), 8)
        slot = a_all.at[origin, 1 - xl, c]
        second.append(net.copy(slot, slot, sib))

    second = []
    pass_on(0)
    forward(0)
    forward(1)
    pass_on(1)

    for copy in small:
        copy.wait_recv()
    pos_rows = jnp.concatenate([pos_all[0, 0] + pos_all[0, 1], pos_all[1, 0] + pos_all[1, 1]], axis=1)
    index = lax.broadcasted_iota(jnp.int32, (64, 256), 0).astype(F32)
    freq = jnp.exp(-jnp.log(F32(1000000.0)) * 2.0 * index / HEAD)
    angle = pos_rows[0:1].astype(F32) * freq
    cosine, sine = jnp.cos(angle), jnp.sin(angle)

    forward(2)
    pass_on(2)
    forward(3)
    pass_on(3)

    for copy in from_y:
        copy.wait_recv()
    m_half[...] = m_own[:, pl.ds(y, 1)].reshape(4, 2, 32, 256) + m_recv[0] + m_recv[1] + m_recv[2]
    xo = net.peer(xh=1)
    from_xh = net.copy(m_half.at[:, xo["xh"]], m_recv2, xo)

    forward(4)
    pass_on(4)

    from_xh.wait_recv()
    m_piece[...] = (m_half[:, pl.ds(xh, 1)].reshape(4, 32, 256) + m_recv2[...]).astype(BF)
    piece = merged.at[y, xh]
    keep_m = pltpu.make_async_copy(m_piece.at[g], piece.at[:, features], local_sem.at[2])
    keep_m.start()
    from_group = []
    for offsets in GROUP:
        p = net.peer(**offsets)
        from_group.append(net.copy(m_piece.at[p["xl"] * 2 + p["c"]], piece.at[:, features], p))

    forward(5)
    pass_on(5)

    keep_m.wait()
    for copy in from_group:
        copy.wait_recv()
    from_xh2 = net.copy(piece, piece, xo)

    forward(6)
    pass_on(6)

    from_xh2.wait_recv()
    from_y2 = []
    for d in (2, 1, 3):
        from_y2.append(net.copy(merged.at[y], merged.at[y], net.peer(y=d)))
    pass_on(7)

    keep.wait()
    keep_tau.wait()
    for copy in from_tau + to_sib + second + from_y2:
        copy.wait_recv()

    def partial_gap(d):
        zd = lax.rem(z + d, 8)
        rows = a_all[pl.ds(zd, 1)].reshape(256, 1024)
        gap[zd] = nt(merged[...].reshape(256, 1024), rows) - nt(tau_t[...], rows)

    sides = ((0, 1), (1, 7))
    from_rs = {}

    def rs_step(step):
        d = 5 - step
        for h in range(2):
            for s, by in sides:
                zd = lax.rem(z + (by * d) % 8, 8)
                half = slice(s * 64, s * 64 + 64)
                out = rs_send.at[h, s, step - 1]
                if step == 1:
                    at = h * 128 + s * 64
                    out[half] = gap[zd, at : at + 64].astype(BF)
                elif step == 2:
                    from_rs[h, s, 1].wait_recv()
                    other = 1 - s
                    at = h * 128 + s * 64
                    out[half] = (
                        gap[zd, at : at + 64] + rs_recv[h, s, 0, half].astype(F32)
                    ).astype(BF)
                    at = h * 128 + other * 64
                    out[other * 64 : other * 64 + 64] = gap[zd, at : at + 64].astype(BF)
                else:
                    from_rs[h, s, step - 1].wait_recv()
                    out[...] = (
                        gap[zd, h * 128 : h * 128 + 128] + rs_recv[h, s, step - 2].astype(F32)
                    ).astype(BF)
                dst = rs_recv.at[h, s, step - 1]
                if step == 1:
                    out, dst = out.at[half], dst.at[half]
                from_rs[h, s, step] = net.copy(out, dst, net.peer(z=by))

    partial_gap(4)
    rs_step(1)
    partial_gap(3)
    partial_gap(5)
    rs_step(2)
    partial_gap(2)
    partial_gap(6)
    rs_step(3)
    partial_gap(1)
    partial_gap(7)
    rs_step(4)
    partial_gap(0)

    lane = lax.broadcasted_iota(jnp.int32, (1, 256), 1)
    row = lax.div(lane, 128) * 1024 + z * 128 + lax.rem(lane, 128)
    count = jnp.full((1, 256), counts[0], jnp.int32)
    live = (row < count).astype(F32)
    scale = 1.0 / (count.astype(F32) * 1024.0)
    weight = 2.0 * scale * live
    squares = jnp.zeros((64, 256), F32)
    from_ag = {}
    for h in range(2):
        for s, _ in sides:
            from_rs[h, s, 4].wait_recv()
        at = h * 128
        full = (
            gap[z, at : at + 128] + rs_recv[h, 0, 3].astype(F32) + rs_recv[h, 1, 3].astype(F32)
        )
        first, second_half = full[0:64], full[64:128]
        err_a = first * cosine - second_half * sine
        err_b = second_half * cosine + first * sine
        squares = squares + (live * err_a * err_a + live * err_b * err_b) * scale
        err_a, err_b = weight * err_a, weight * err_b
        back[z, at : at + 64] = (err_a * cosine + err_b * sine).astype(BF)
        back[z, at + 64 : at + 128] = (err_b * cosine - err_a * sine).astype(BF)
        slot = back.at[z, at : at + 128]
        for s, by in sides:
            from_ag[h, s, 1] = net.copy(slot, slot, net.peer(z=by))

    def tile_of(value):
        return jnp.broadcast_to(value, (8, 128))

    loss_z[z] = tile_of(jnp.sum(squares, keepdims=True))
    small_z = [net.copy(loss_z.at[z], loss_z.at[z], net.peer(z=d)) for d in RING]

    def add_wgrad(d):
        zo = lax.rem(z + d, 8)
        rows = a_all[pl.ds(zo, 1)].reshape(256, 1024)
        term = jnp.dot(back[zo], rows, preferred_element_type=F32)
        if d == 0:
            w_acc[...] = term
        else:
            w_acc[...] += term

    for step in range(2, 5):
        for h in range(2):
            for s, by in sides:
                from_ag[h, s, step - 1].wait_recv()
                zo = lax.rem(z + (-by * (step - 1)) % 8, 8)
                at = h * 128
                slot = back.at[zo, at : at + 128]
                if step == 4:
                    slot = back.at[zo, at + s * 64 : at + s * 64 + 64]
                from_ag[h, s, step] = net.copy(slot, slot, net.peer(z=by))
        if step == 2:
            add_wgrad(0)
        add_wgrad(step - 1)
        add_wgrad(9 - step)

    for copy in small_z:
        copy.wait_recv()
    loss_g[g] = jnp.sum(loss_z[...], axis=0)
    small_g = [net.copy(loss_g.at[g], loss_g.at[g], net.peer(**o)) for o in GROUP]

    for h in range(2):
        for s, _ in sides:
            from_ag[h, s, 4].wait_recv()
    add_wgrad(4)

    w_send[...] = w_acc[...].reshape(8, 32, 1024).astype(BF)
    from_t = []
    for i, (a, b) in enumerate(TASKS):
        p = net.peer(xh=a, y=b)
        from_t.append(net.copy(w_send.at[p["xh"] * 4 + p["y"]], w_recv.at[i], p))
    for copy in small_g:
        copy.wait_recv()
    loss_t[t] = jnp.sum(loss_g[...], axis=0)
    small_t = [
        net.copy(loss_t.at[t], loss_t.at[t], net.peer(xh=a, y=b)) for a, b in TASKS
    ]
    summed = w_acc[pl.ds(pl.multiple_of(t * 32, 32), 32)]
    for i, copy in enumerate(from_t):
        copy.wait_recv()
        summed = summed + w_recv[i].astype(F32)
    for k in range(4):
        w_piece[k] = summed[:, k * 256 : (k + 1) * 256].astype(BF)
    mine = w_all.at[:, t]
    keep_w = pltpu.make_async_copy(w_piece.at[g], w_all.at[g, t], local_sem.at[3])
    keep_w.start()
    from_w = []
    for offsets in GROUP:
        p = net.peer(**offsets)
        from_w.append(net.copy(w_piece.at[p["xl"] * 2 + p["c"]], w_all.at[g, t], p))
    keep_w.wait()
    for copy in from_w:
        copy.wait_recv()
    from_w2 = [net.copy(mine, mine, net.peer(xh=a, y=b)) for a, b in TASKS]
    for copy in small_t:
        copy.wait_recv()
    loss_out[...] = jnp.sum(loss_t[...], axis=0)
    for copy in from_w2:
        copy.wait_recv()
    for k in range(8):
        block = w_all[k // 2, 4 * (k % 2) : 4 * (k % 2) + 4].reshape(128, 256)
        w_out[:, k * 128 : (k + 1) * 128] = block.astype(F32).T

    net.drain()


def local(hidden, gain, tau, coeff, counts, positions):
    vmem = pl.BlockSpec(memory_space=pltpu.VMEM)
    w, loss = pl.pallas_call(
        kernel,
        out_shape=(
            jax.ShapeDtypeStruct((256, 1024), F32),
            jax.ShapeDtypeStruct((8, 128), F32),
        ),
        in_specs=[pl.BlockSpec(memory_space=pltpu.SMEM)] + [vmem] * 5,
        out_specs=(vmem, vmem),
        scratch_shapes=[
            pltpu.VMEM((8, 64, 1024), BF),
            pltpu.VMEM((8, 2, 2, 64, 1024), BF),
            pltpu.VMEM((4, 256, 256), BF),
            pltpu.VMEM((256, 1024), BF),
            pltpu.VMEM((4, 4, 2, 32, 256), F32),
            pltpu.VMEM((3, 4, 2, 32, 256), F32),
            pltpu.VMEM((4, 2, 32, 256), F32),
            pltpu.VMEM((4, 32, 256), F32),
            pltpu.VMEM((4, 32, 256), BF),
            pltpu.VMEM((4, 2, 32, 1024), BF),
            pltpu.VMEM((8, 256, 256), F32),
            pltpu.VMEM((2, 2, 4, 128, 256), BF),
            pltpu.VMEM((2, 2, 4, 128, 256), BF),
            pltpu.VMEM((8, 256, 256), BF),
            pltpu.VMEM((256, 1024), F32),
            pltpu.VMEM((8, 32, 1024), BF),
            pltpu.VMEM((7, 32, 1024), BF),
            pltpu.VMEM((4, 32, 256), BF),
            pltpu.VMEM((4, 8, 32, 256), BF),
            pltpu.VMEM((2, 2, 8, 128), jnp.int32),
            pltpu.VMEM((8, 8, 128), F32),
            pltpu.VMEM((4, 8, 128), F32),
            pltpu.VMEM((8, 8, 128), F32),
            pltpu.SemaphoreType.DMA((N_SEM,)),
            pltpu.SemaphoreType.DMA((N_SEM,)),
            pltpu.SemaphoreType.DMA((4,)),
        ],
        compiler_params=pltpu.CompilerParams(
            collective_id=0, has_side_effects=True, vmem_limit_bytes=56 * 2**20
        ),
        name="step",
    )(
        counts,
        hidden[0],
        gain.reshape(1, -1),
        tau[0],
        coeff[0],
        jnp.concatenate([positions, positions], axis=1),
    )
    grad = 8192 * 1024 * tau[0].astype(F32) * w
    return grad[None], loss[0, 0]


def solution(mesh):
    spec = P("task", "mp", None)
    return jax.shard_map(
        local,
        mesh=mesh,
        in_specs=(spec, P(), spec, spec, P("task"), P("task", "mp")),
        out_specs=(spec, P()),
        check_vma=False,
    )
```

```python
import jax
import jax.numpy as jnp
from jax import lax
from jax.experimental import pallas as pl
from jax.experimental.pallas import tpu as pltpu
from jax.sharding import PartitionSpec as P

MESH = pl.DeviceIdType.MESH
BF = jnp.bfloat16
F32 = jnp.float32
HEAD = 128
SIZES = dict(xh=2, y=4, xl=2, z=8, c=2)
GROUP = (dict(c=1), dict(xl=1), dict(xl=1, c=1))
EIGHT = GROUP + tuple(dict(xh=1, **o) for o in (dict(),) + GROUP)
TASKS = tuple(dict(xh=a, y=b) for a in (1, 0) for b in (2, 1, 3, 0) if (a, b) != (0, 0))
RING = (4, 3, 5, 2, 6, 1, 7)
N_SEM = 192


class Links:
    def __init__(self, here, send, recv):
        self.here, self.send, self.recv, self.used, self.open = here, send, recv, 0, []

    def peer(self, **offsets):
        p = dict(self.here)
        for axis, by in offsets.items():
            p[axis] = lax.rem(p[axis] + (by % SIZES[axis]), SIZES[axis])
        return p

    def device(self, p):
        return (p["xh"] * 4 + p["y"], p["xl"] * 16 + p["z"] * 2 + p["c"])

    def copy(self, src, dst, p):
        i = self.used
        self.used += 1
        made = pltpu.make_async_remote_copy(
            src_ref=src,
            dst_ref=dst,
            send_sem=self.send.at[i],
            recv_sem=self.recv.at[i],
            device_id=self.device(p),
            device_id_type=MESH,
        )
        made.start()
        self.open.append(made)
        return made

    def drain(self):
        for made in self.open:
            made.wait_send()


def nt(a, b):
    return lax.dot_general(a, b, (((1,), (1,)), ((), ())), preferred_element_type=F32)


def kernel(
    counts,
    hidden_hbm,
    gain,
    tau_hbm,
    coeff_hbm,
    pos,
    out_hbm,
    loss_out,
    hidden,
    tau,
    coeff,
    ns,
    a_all,
    tau_own,
    tau_t,
    m_own,
    m_recv,
    m_half,
    m_recv2,
    m_piece,
    merged,
    gap,
    rs_send,
    rs_recv,
    back,
    w_acc,
    w_send,
    w_recv,
    w_piece,
    w_all,
    grad,
    pos_all,
    loss_z,
    loss_g,
    loss_t,
    send_sem,
    recv_sem,
    local_sem,
):
    loads = [
        pltpu.make_async_copy(src, dst, local_sem.at[i])
        for i, (src, dst) in enumerate(((tau_hbm, tau), (coeff_hbm, coeff), (hidden_hbm, hidden)))
    ]
    for load in loads:
        load.start()

    t, m = lax.axis_index("task"), lax.axis_index("mp")
    me = dict(
        xh=lax.div(t, 4),
        y=lax.rem(t, 4),
        xl=lax.div(m, 16),
        z=lax.rem(lax.div(m, 2), 8),
        c=lax.rem(m, 2),
    )
    net = Links(me, send_sem, recv_sem)
    xl, z, c, y, xh = me["xl"], me["z"], me["c"], me["y"], me["xh"]
    g = xl * 2 + c

    barrier = pltpu.get_barrier_semaphore()
    partners = [dict(z=d) for d in RING] + list(EIGHT) + [o for o in TASKS if "y" in o and o["y"]]
    for offsets in partners:
        pl.semaphore_signal(
            barrier, inc=1, device_id=net.device(net.peer(**offsets)), device_id_type=MESH
        )

    loads[0].wait()
    loads[1].wait()
    for k in range(8):
        cut = slice(k * 128, (k + 1) * 128)
        tau_f = tau[:, cut].astype(F32)
        mixed_t = (coeff[:, cut] * tau_f).T
        m_own[k // 2, 2 * (k % 2) : 2 * (k % 2) + 2] = mixed_t.reshape(2, 2, 32, 256)
        tau_own[k // 2, (k % 2) * 128 : (k % 2) * 128 + 128] = tau_f.T.astype(BF)

    loads[2].wait()
    total = jnp.zeros((64, 128), F32)
    for k in range(64):
        x = hidden[:, k * 128 : (k + 1) * 128].astype(F32)
        total = total + x * x
    inverse = 1.0 / jnp.sqrt(jnp.sum(total, axis=1, keepdims=True) * (1.0 / 8192.0) + 1e-06)
    inverse = jnp.broadcast_to(inverse, (64, 128))
    for k in range(8):
        for half in range(2):
            for part in range(4):
                at = half * 4096 + k * 512 + part * 128
                x = hidden[:, at : at + 128].astype(F32)
                to = half * 512 + part * 128
                ns[k, :, to : to + 128] = (x * inverse * gain[:, at : at + 128]).astype(BF)

    pl.semaphore_wait(barrier, len(partners))

    from_y = []
    for i, d in enumerate((2, 1, 3)):
        p = net.peer(y=d)
        from_y.append(net.copy(m_own.at[:, p["y"]], m_recv.at[i], p))

    from_z = []
    for d in RING:
        p = net.peer(z=d)
        from_z.append(net.copy(ns.at[p["z"]], a_all.at[z, xl, c], p))
    sib, xn = net.peer(c=1), net.peer(xl=1)
    own_slot = a_all.at[z, xl, c]
    keep = pltpu.make_async_copy(ns.at[z], own_slot, local_sem.at[3])
    keep.start()
    to_sib, to_x, second = [], [], []
    to_sib.append(net.copy(ns.at[z], own_slot, sib))
    to_x.append(net.copy(ns.at[z], own_slot, xn))

    features = pl.ds(pl.multiple_of(g * 256, 256), 256)
    from_tau = []
    for offsets in GROUP:
        p = net.peer(**offsets)
        from_tau.append(net.copy(tau_own.at[p["xl"] * 2 + p["c"]], tau_t.at[:, features], p))
    keep_tau = pltpu.make_async_copy(tau_own.at[g], tau_t.at[:, features], local_sem.at[4])
    keep_tau.start()

    lanes = lax.broadcasted_iota(jnp.int32, (8, 128), 1)
    twice = jnp.concatenate([pos[...], pos[...]], axis=1)
    pos_all[xl, c] = jnp.where(lax.div(lanes, 64) == c, jnp.broadcast_to(twice, (8, 128)), 0)
    small = []
    for offsets in GROUP:
        small.append(net.copy(pos_all.at[xl, c], pos_all.at[xl, c], net.peer(**offsets)))

    def forward(i):
        from_z[i].wait_recv()
        slot = a_all.at[lax.rem(z + (8 - RING[i]), 8), xl, c]
        to_sib.append(net.copy(slot, slot, sib))
        to_x.append(net.copy(slot, slot, xn))

    def pass_on(i):
        to_x[i].wait_recv()
        origin = z if i == 0 else lax.rem(z + (8 - RING[i - 1]), 8)
        slot = a_all.at[origin, 1 - xl, c]
        second.append(net.copy(slot, slot, sib))

    forward(0)
    pass_on(0)

    for copy in small:
        copy.wait_recv()
    halves = (xl, 1 - xl)
    index = lax.broadcasted_iota(jnp.int32, (64, 128), 0).astype(F32)
    freq = jnp.exp(-jnp.log(F32(1000000.0)) * 2.0 * index / HEAD)
    cosine, sine = [], []
    for xr in halves:
        at_rows = pos_all[xr, 0] + pos_all[xr, 1]
        angle = at_rows[0:1].astype(F32) * freq
        cosine.append(jnp.cos(angle))
        sine.append(jnp.sin(angle))

    forward(1)
    forward(2)
    pass_on(1)

    for copy in from_y:
        copy.wait_recv()
    m_half[...] = m_own[:, pl.ds(y, 1)].reshape(4, 2, 32, 256) + m_recv[0] + m_recv[1] + m_recv[2]
    xo = net.peer(xh=1)
    from_xh = net.copy(m_half.at[:, xo["xh"]], m_recv2, xo)

    forward(3)
    pass_on(2)
    pass_on(3)

    from_xh.wait_recv()
    m_piece[...] = (m_half[:, pl.ds(xh, 1)].reshape(4, 32, 256) + m_recv2[...]).astype(BF)
    piece = merged.at[y, xh, :, features]
    keep_m = pltpu.make_async_copy(m_piece.at[g], piece, local_sem.at[5])
    keep_m.start()
    from_eight = []
    for offsets in EIGHT:
        p = net.peer(**offsets)
        from_eight.append(net.copy(m_piece.at[p["xl"] * 2 + p["c"]], piece, p))

    forward(4)
    pass_on(4)

    keep_m.wait()
    for copy in from_eight:
        copy.wait_recv()
    from_y2 = []
    for d in (2, 1, 3):
        from_y2.append(net.copy(merged.at[y], merged.at[y], net.peer(y=d)))

    forward(5)
    pass_on(5)
    forward(6)
    pass_on(6)

    keep.wait()
    keep_tau.wait()
    for copy in from_tau + to_sib + from_y2:
        copy.wait_recv()

    def partial_gap(d, rh):
        zd = lax.rem(z + d, 8)
        rows = a_all[pl.ds(zd, 1), pl.ds(halves[rh], 1)].reshape(128, 1024)
        gap[zd, rh] = nt(merged[...].reshape(256, 1024), rows) - nt(tau_t[...], rows)

    sides = ((0, 1), (1, 7))
    from_rs = {}

    def rs_step(step, rh):
        d = 5 - step
        for h in range(2):
            for s, by in sides:
                zd = lax.rem(z + (by * d) % 8, 8)
                half = slice(s * 64, s * 64 + 64)
                other = slice(64 - s * 64, 128 - s * 64)
                terms = gap[zd, rh, h * 128 : h * 128 + 128]
                out = rs_send.at[rh, h, s, step - 1]
                if step > 1:
                    from_rs[rh, h, s, step - 1].wait_recv()
                came = rs_recv.at[rh, h, s, step - 2]
                if step == 1:
                    out[half] = terms[half].astype(BF)
                elif step == 2:
                    out[half] = (terms[half] + came[half].astype(F32)).astype(BF)
                    out[other] = terms[other].astype(BF)
                else:
                    out[...] = (terms + came[...].astype(F32)).astype(BF)
                dst = rs_recv.at[rh, h, s, step - 1]
                if step == 1:
                    out, dst = out.at[half], dst.at[half]
                from_rs[rh, h, s, step] = net.copy(out, dst, net.peer(z=by))

    partial_gap(4, 0)
    rs_step(1, 0)
    pass_on(7)
    for copy in second:
        copy.wait_recv()
    partial_gap(4, 1)
    rs_step(1, 1)
    for step in (2, 3, 4):
        for rh in range(2):
            partial_gap(5 - step, rh)
            partial_gap(3 + step, rh)
            rs_step(step, rh)
    partial_gap(0, 0)
    partial_gap(0, 1)

    squares = jnp.zeros((64, 128), F32)
    lane = lax.broadcasted_iota(jnp.int32, (1, 128), 1)
    count = jnp.full((1, 128), counts[0], jnp.int32)
    scale = 1.0 / (count.astype(F32) * 1024.0)
    from_ag = {}
    for rh in range(2):
        row = halves[rh] * 1024 + z * 128 + lane
        live = (row < count).astype(F32)
        weight = 2.0 * scale * live
        for h in range(2):
            for s, _ in sides:
                from_rs[rh, h, s, 4].wait_recv()
            at = h * 128
            full = (
                gap[z, rh, at : at + 128]
                + rs_recv[rh, h, 0, 3].astype(F32)
                + rs_recv[rh, h, 1, 3].astype(F32)
            )
            first, last = full[0:64], full[64:128]
            err_a = first * cosine[rh] - last * sine[rh]
            err_b = last * cosine[rh] + first * sine[rh]
            squares = squares + (live * err_a * err_a + live * err_b * err_b) * scale
            err_a, err_b = weight * err_a, weight * err_b
            slot = back.at[z, halves[rh], at : at + 128]
            slot[0:64] = (err_a * cosine[rh] + err_b * sine[rh]).astype(BF)
            slot[64:128] = (err_b * cosine[rh] - err_a * sine[rh]).astype(BF)
            for s, by in sides:
                from_ag[rh, h, s, 1] = net.copy(slot, slot, net.peer(z=by))

    def tile_of(value):
        return jnp.broadcast_to(value, (8, 128))

    loss_z[z] = tile_of(jnp.sum(squares, keepdims=True))
    small_z = [net.copy(loss_z.at[z], loss_z.at[z], net.peer(z=d)) for d in RING]

    def add_wgrad(d):
        zo = lax.rem(z + d, 8)
        rows = a_all[pl.ds(zo, 1)].reshape(256, 1024)
        errors = jnp.concatenate([back[zo, 0], back[zo, 1]], axis=1)
        term = jnp.dot(errors, rows, preferred_element_type=F32)
        if d == 0:
            w_acc[...] = term
        else:
            w_acc[...] += term

    for step in range(2, 5):
        for rh in range(2):
            for h in range(2):
                for s, by in sides:
                    from_ag[rh, h, s, step - 1].wait_recv()
                    zo = lax.rem(z + (-by * (step - 1)) % 8, 8)
                    at, size = h * 128, 128
                    if step == 4:
                        at, size = at + s * 64, 64
                    slot = back.at[zo, halves[rh], at : at + size]
                    from_ag[rh, h, s, step] = net.copy(slot, slot, net.peer(z=by))
        if step == 2:
            add_wgrad(0)
        add_wgrad(step - 1)
        add_wgrad(9 - step)

    for copy in small_z:
        copy.wait_recv()
    loss_g[g] = jnp.sum(loss_z[...], axis=0)
    small_g = [net.copy(loss_g.at[g], loss_g.at[g], net.peer(**o)) for o in GROUP]

    for rh in range(2):
        for h in range(2):
            for s, _ in sides:
                from_ag[rh, h, s, 4].wait_recv()
    add_wgrad(4)

    w_send[...] = w_acc[...].reshape(2, 8, 16, 1024).astype(BF)
    from_t, from_w, from_w2, keep_w = [], [], [], []
    for h in range(2):
        for i, offsets in enumerate(TASKS):
            p = net.peer(**offsets)
            from_t.append(net.copy(w_send.at[h, p["xh"] * 4 + p["y"]], w_recv.at[h, i], p))
    for copy in small_g:
        copy.wait_recv()
    loss_t[t] = jnp.sum(loss_g[...], axis=0)
    small_t = [net.copy(loss_t.at[t], loss_t.at[t], net.peer(**o)) for o in TASKS]
    for h in range(2):
        summed = w_acc[pl.ds(pl.multiple_of(h * 128 + t * 16, 16), 16)]
        for i in range(7):
            from_t[h * 7 + i].wait_recv()
            summed = summed + w_recv[h, i].astype(F32)
        for k in range(4):
            w_piece[h, k] = summed[:, k * 256 : (k + 1) * 256].astype(BF)
        keep_w.append(
            pltpu.make_async_copy(w_piece.at[h, g], w_all.at[g, h, t], local_sem.at[6 + h])
        )
        keep_w[h].start()
        for offsets in GROUP:
            p = net.peer(**offsets)
            from_w.append(
                net.copy(w_piece.at[h, p["xl"] * 2 + p["c"]], w_all.at[g, h, t], p)
            )
    for h in range(2):
        keep_w[h].wait()
        for i in range(3):
            from_w[h * 3 + i].wait_recv()
        mine = w_all.at[:, h, t]
        for offsets in TASKS:
            from_w2.append(net.copy(mine, mine, net.peer(**offsets)))
    for copy in small_t:
        copy.wait_recv()
    loss_out[...] = jnp.sum(loss_t[...], axis=0)[0:1, 0:1]
    stores = []
    for h in range(2):
        for i in range(7):
            from_w2[h * 7 + i].wait_recv()
        for k in range(4):
            cut = slice(k * 256 + h * 128, k * 256 + h * 128 + 128)
            block = w_all[k, h].reshape(128, 256).astype(F32).T
            grad[:, cut] = (8192 * 1024) * tau[:, cut].astype(F32) * block
            store = pltpu.make_async_copy(
                grad.at[:, cut], out_hbm.at[:, cut], local_sem.at[8 + h * 4 + k]
            )
            store.start()
            stores.append(store)
    for store in stores:
        store.wait()
    net.drain()


def local(hidden, gain, tau, coeff, counts, positions):
    vmem = pl.BlockSpec(memory_space=pltpu.VMEM)
    hbm = pl.BlockSpec(memory_space=pl.ANY)
    grad, loss = pl.pallas_call(
        kernel,
        out_shape=(
            jax.ShapeDtypeStruct((256, 1024), F32),
            jax.ShapeDtypeStruct((1, 1), F32),
        ),
        in_specs=[pl.BlockSpec(memory_space=pltpu.SMEM), hbm, vmem, hbm, hbm, vmem],
        out_specs=(hbm, vmem),
        scratch_shapes=[
            pltpu.VMEM((64, 8192), BF),
            pltpu.VMEM((256, 1024), BF),
            pltpu.VMEM((256, 1024), F32),
            pltpu.VMEM((8, 64, 1024), BF),
            pltpu.VMEM((8, 2, 2, 64, 1024), BF),
            pltpu.VMEM((4, 256, 256), BF),
            pltpu.VMEM((256, 1024), BF),
            pltpu.VMEM((4, 4, 2, 32, 256), F32),
            pltpu.VMEM((3, 4, 2, 32, 256), F32),
            pltpu.VMEM((4, 2, 32, 256), F32),
            pltpu.VMEM((4, 32, 256), F32),
            pltpu.VMEM((4, 32, 256), BF),
            pltpu.VMEM((4, 2, 32, 1024), BF),
            pltpu.VMEM((8, 2, 256, 128), F32),
            pltpu.VMEM((2, 2, 2, 4, 128, 128), BF),
            pltpu.VMEM((2, 2, 2, 4, 128, 128), BF),
            pltpu.VMEM((8, 2, 256, 128), BF),
            pltpu.VMEM((256, 1024), F32),
            pltpu.VMEM((2, 8, 16, 1024), BF),
            pltpu.VMEM((2, 7, 16, 1024), BF),
            pltpu.VMEM((2, 4, 16, 256), BF),
            pltpu.VMEM((4, 2, 8, 16, 256), BF),
            pltpu.VMEM((256, 1024), F32),
            pltpu.VMEM((2, 2, 8, 128), jnp.int32),
            pltpu.VMEM((8, 8, 128), F32),
            pltpu.VMEM((4, 8, 128), F32),
            pltpu.VMEM((8, 8, 128), F32),
            pltpu.SemaphoreType.DMA((N_SEM,)),
            pltpu.SemaphoreType.DMA((N_SEM,)),
            pltpu.SemaphoreType.DMA((16,)),
        ],
        compiler_params=pltpu.CompilerParams(
            collective_id=0, has_side_effects=True, vmem_limit_bytes=56 * 2**20
        ),
        name="step",
    )(counts, hidden[0], gain.reshape(1, -1), tau[0], coeff[0], positions)
    return grad[None], loss[0, 0]


def solution(mesh):
    spec = P("task", "mp", None)
    return jax.shard_map(
        local,
        mesh=mesh,
        in_specs=(spec, P(), spec, spec, P("task"), P("task", "mp")),
        out_specs=(spec, P()),
        check_vma=False,
    )
```

```python
import jax
import jax.numpy as jnp
from jax import lax
from jax.experimental import pallas as pl
from jax.experimental.pallas import tpu as pltpu
from jax.sharding import PartitionSpec as P

MESH = pl.DeviceIdType.MESH
BF = jnp.bfloat16
F32 = jnp.float32
HEAD = 128
SIZES = dict(xh=2, y=4, xl=2, z=8, c=2)
GROUP = (dict(c=1), dict(xl=1), dict(xl=1, c=1))
EIGHT = GROUP + tuple(dict(xh=1, **o) for o in (dict(),) + GROUP)
TASKS = tuple(dict(xh=a, y=b) for a in (1, 0) for b in (2, 1, 3, 0) if (a, b) != (0, 0))
PLANE = tuple(
    dict(xh=a, y=b, xl=k, c=d)
    for a in (1, 0)
    for b in (2, 1, 3, 0)
    for k in (1, 0)
    for d in (0, 1)
    if (a, b, k, d) != (0, 0, 0, 0)
)
RING = (1, 7, 2, 6, 3, 5, 4)
N_SEM = 192

FIRST = 4
ORDER = (
    ('q', 0),
    ('q', 1),
    ('s', 4),
    ('s', 5),
    ('f', 0),
    ('f', 1),
    ('t',),
    ('q', 2),
    ('q', 3),
    ('s', 6),
    ('y',),
    ('f', 2),
    ('f', 3),
    ('e',),
    ('p', 0),
    ('p', 1),
    ('p', 2),
    ('q', 4),
    ('q', 5),
    ('f', 4),
    ('f', 5),
    ('q', 6),
    ('f', 6),
)
RSORDER = ("a1", "P", "b1", "a2", "b2", "a3", "b3", "a4", "b4")


class Links:
    def __init__(self, here, send, recv):
        self.here, self.send, self.recv, self.used, self.open = here, send, recv, 0, []

    def peer(self, **offsets):
        p = dict(self.here)
        for axis, by in offsets.items():
            p[axis] = lax.rem(p[axis] + (by % SIZES[axis]), SIZES[axis])
        return p

    def device(self, p):
        return (p["xh"] * 4 + p["y"], p["xl"] * 16 + p["z"] * 2 + p["c"])

    def copy(self, src, dst, p):
        i = self.used
        self.used += 1
        made = pltpu.make_async_remote_copy(
            src_ref=src,
            dst_ref=dst,
            send_sem=self.send.at[i],
            recv_sem=self.recv.at[i],
            device_id=self.device(p),
            device_id_type=MESH,
        )
        made.start()
        self.open.append(made)
        return made

    def drain(self):
        for made in self.open:
            made.wait_send()


def nt(a, b):
    return lax.dot_general(a, b, (((1,), (1,)), ((), ())), preferred_element_type=F32)


def kernel(
    counts,
    hidden_hbm,
    gain,
    tau_hbm,
    coeff_hbm,
    pos,
    out_hbm,
    loss_out,
    hidden,
    tau,
    coeff,
    ns,
    a_all,
    tau_own,
    tau_t,
    m_own,
    m_recv,
    m_half,
    m_recv2,
    merged,
    gap,
    rs_send,
    rs_recv,
    back,
    w_acc,
    w_send,
    w_recv,
    w_all,
    grad,
    pos_all,
    loss_z,
    loss_g,
    loss_t,
    send_sem,
    recv_sem,
    local_sem,
):
    loads = [
        pltpu.make_async_copy(src, dst, local_sem.at[i])
        for i, (src, dst) in enumerate(((tau_hbm, tau), (coeff_hbm, coeff), (hidden_hbm, hidden)))
    ]
    for load in loads:
        load.start()

    t, m = lax.axis_index("task"), lax.axis_index("mp")
    me = dict(
        xh=lax.div(t, 4),
        y=lax.rem(t, 4),
        xl=lax.div(m, 16),
        z=lax.rem(lax.div(m, 2), 8),
        c=lax.rem(m, 2),
    )
    net = Links(me, send_sem, recv_sem)
    xl, z, c, y, xh = me["xl"], me["z"], me["c"], me["y"], me["xh"]
    g = xl * 2 + c

    barrier = pltpu.get_barrier_semaphore()
    partners = [dict(z=d) for d in RING] + list(PLANE)
    for offsets in partners:
        pl.semaphore_signal(
            barrier, inc=1, device_id=net.device(net.peer(**offsets)), device_id_type=MESH
        )

    loads[0].wait()
    loads[1].wait()
    for k in range(8):
        cut = slice(k * 128, (k + 1) * 128)
        tau_f = tau[:, cut].astype(F32)
        mixed_t = (coeff[:, cut] * tau_f).T
        m_own[k // 2, 2 * (k % 2) : 2 * (k % 2) + 2] = mixed_t.reshape(2, 2, 32, 256)
        tau_own[k // 2, (k % 2) * 128 : (k % 2) * 128 + 128] = tau_f.T.astype(BF)

    loads[2].wait()
    total = jnp.zeros((64, 128), F32)
    for k in range(64):
        x = hidden[:, k * 128 : (k + 1) * 128].astype(F32)
        total = total + x * x
    inverse = 1.0 / jnp.sqrt(jnp.sum(total, axis=1, keepdims=True) * (1.0 / 8192.0) + 1e-06)
    inverse = jnp.broadcast_to(inverse, (64, 128))
    for k in range(8):
        for half in range(2):
            for part in range(4):
                at = half * 4096 + k * 512 + part * 128
                x = hidden[:, at : at + 128].astype(F32)
                to = half * 512 + part * 128
                ns[k, :, to : to + 128] = (x * inverse * gain[:, at : at + 128]).astype(BF)

    pl.semaphore_wait(barrier, len(partners))

    from_y = []
    for i, d in enumerate((2, 1, 3)):
        p = net.peer(y=d)
        from_y.append(net.copy(m_own.at[:, p["y"]], m_recv.at[i], p))

    from_z = []

    def send_z(i):
        p = net.peer(z=RING[i])
        from_z.append(net.copy(ns.at[p["z"]], a_all.at[z, xl, c], p))

    for i in range(FIRST):
        send_z(i)
    sib, xn = net.peer(c=1), net.peer(xl=1)
    own_slot = a_all.at[z, xl, c]
    keep = pltpu.make_async_copy(ns.at[z], own_slot, local_sem.at[3])
    keep.start()
    to_sib, to_x, second = [], [], []
    to_sib.append(net.copy(ns.at[z], own_slot, sib))
    to_x.append(net.copy(ns.at[z], own_slot, xn))

    features = pl.ds(pl.multiple_of(g * 256, 256), 256)
    from_tau = []
    for offsets in GROUP:
        p = net.peer(**offsets)
        from_tau.append(net.copy(tau_own.at[p["xl"] * 2 + p["c"]], tau_t.at[:, features], p))
    keep_tau = pltpu.make_async_copy(tau_own.at[g], tau_t.at[:, features], local_sem.at[4])
    keep_tau.start()

    lanes = lax.broadcasted_iota(jnp.int32, (8, 128), 1)
    twice = jnp.concatenate([pos[...], pos[...]], axis=1)
    pos_all[xl, c] = jnp.where(lax.div(lanes, 64) == c, jnp.broadcast_to(twice, (8, 128)), 0)
    small = []
    for offsets in GROUP:
        small.append(net.copy(pos_all.at[xl, c], pos_all.at[xl, c], net.peer(**offsets)))

    def slot_of(i):
        return a_all.at[lax.rem(z + (8 - RING[i]), 8), xl, c]

    def arrived(i):
        from_z[i].wait_recv()
        to_sib.append(net.copy(slot_of(i), slot_of(i), sib))

    def forward(i):
        to_x.append(net.copy(slot_of(i), slot_of(i), xn))

    def pass_on(i):
        to_x[i].wait_recv()
        origin = z if i == 0 else lax.rem(z + (8 - RING[i - 1]), 8)
        slot = a_all.at[origin, 1 - xl, c]
        second.append(net.copy(slot, slot, sib))

    halves = (xl, 1 - xl)
    cosine, sine = [], []
    from_y2, from_eight = [], []

    def tables():
        for copy in small:
            copy.wait_recv()
        index = lax.broadcasted_iota(jnp.int32, (64, 128), 0).astype(F32)
        freq = jnp.exp(-jnp.log(F32(1000000.0)) * 2.0 * index / HEAD)
        for xr in halves:
            at_rows = pos_all[xr, 0] + pos_all[xr, 1]
            angle = at_rows[0:1].astype(F32) * freq
            cosine.append(jnp.cos(angle))
            sine.append(jnp.sin(angle))

    def sum_y():
        for copy in from_y:
            copy.wait_recv()
        m_half[...] = (
            m_own[:, pl.ds(y, 1)].reshape(4, 2, 32, 256) + m_recv[0] + m_recv[1] + m_recv[2]
        )
        m_recv2[xh, g] = m_half[g]
        for offsets in EIGHT:
            p = net.peer(**offsets)
            from_eight.append(net.copy(m_half.at[p["xl"] * 2 + p["c"]], m_recv2.at[xh, g], p))

    def spread_y():
        for copy in from_eight:
            copy.wait_recv()
        for k in range(4):
            merged[y, :, :, k * 256 : (k + 1) * 256] = (m_recv2[0, k] + m_recv2[1, k]).astype(BF)
        for d in (2, 1, 3):
            from_y2.append(net.copy(merged.at[y], merged.at[y], net.peer(y=d)))

    for what, *i in ORDER:
        dict(f=forward, q=arrived, p=pass_on, t=tables, y=sum_y, e=spread_y, s=send_z)[what](*i)

    keep.wait()
    keep_tau.wait()
    for copy in from_tau + to_sib + from_y2:
        copy.wait_recv()

    def partial_gap(d, rh):
        zd = lax.rem(z + d, 8)
        rows = a_all[pl.ds(zd, 1), pl.ds(halves[rh], 1)].reshape(128, 1024)
        gap[zd, rh] = nt(merged[...].reshape(256, 1024), rows) - nt(tau_t[...], rows)

    sides = ((0, 1), (1, 7))
    from_rs = {}

    def rs_step(step, rh):
        d = 5 - step
        for h in range(2):
            for s, by in sides:
                zd = lax.rem(z + (by * d) % 8, 8)
                half = slice(s * 64, s * 64 + 64)
                other = slice(64 - s * 64, 128 - s * 64)
                terms = gap[zd, rh, h * 128 : h * 128 + 128]
                out = rs_send.at[rh, h, s, step - 1]
                if step > 1:
                    from_rs[rh, h, s, step - 1].wait_recv()
                came = rs_recv.at[rh, h, s, step - 2]
                if step == 1:
                    out[half] = terms[half].astype(BF)
                elif step == 2:
                    out[half] = (terms[half] + came[half].astype(F32)).astype(BF)
                    out[other] = terms[other].astype(BF)
                else:
                    out[...] = (terms + came[...].astype(F32)).astype(BF)
                dst = rs_recv.at[rh, h, s, step - 1]
                if step == 1:
                    out, dst = out.at[half], dst.at[half]
                from_rs[rh, h, s, step] = net.copy(out, dst, net.peer(z=by))

    def step_of(step, rh):
        partial_gap(5 - step, rh)
        if step > 1:
            partial_gap(3 + step, rh)
        rs_step(step, rh)

    for what in RSORDER:
        if what == "P":
            for i in range(len(second), 8):
                pass_on(i)
            for copy in second:
                copy.wait_recv()
        else:
            step_of(int(what[1]), "ab".index(what[0]))
    partial_gap(0, 0)
    partial_gap(0, 1)

    squares = jnp.zeros((64, 128), F32)
    lane = lax.broadcasted_iota(jnp.int32, (1, 128), 1)
    count = jnp.full((1, 128), counts[0], jnp.int32)
    scale = 1.0 / (count.astype(F32) * 1024.0)
    from_ag = {}
    for rh in range(2):
        row = halves[rh] * 1024 + z * 128 + lane
        live = (row < count).astype(F32)
        weight = 2.0 * scale * live
        for h in range(2):
            for s, _ in sides:
                from_rs[rh, h, s, 4].wait_recv()
            at = h * 128
            full = (
                gap[z, rh, at : at + 128]
                + rs_recv[rh, h, 0, 3].astype(F32)
                + rs_recv[rh, h, 1, 3].astype(F32)
            )
            first, last = full[0:64], full[64:128]
            err_a = first * cosine[rh] - last * sine[rh]
            err_b = last * cosine[rh] + first * sine[rh]
            squares = squares + (live * err_a * err_a + live * err_b * err_b) * scale
            err_a, err_b = weight * err_a, weight * err_b
            slot = back.at[z, halves[rh], at : at + 128]
            slot[0:64] = (err_a * cosine[rh] + err_b * sine[rh]).astype(BF)
            slot[64:128] = (err_b * cosine[rh] - err_a * sine[rh]).astype(BF)
            for s, by in sides:
                from_ag[rh, h, s, 1] = net.copy(slot, slot, net.peer(z=by))

    def tile_of(value):
        return jnp.broadcast_to(value, (8, 128))

    loss_z[z] = tile_of(jnp.sum(squares, keepdims=True))
    small_z = [net.copy(loss_z.at[z], loss_z.at[z], net.peer(z=d)) for d in RING]

    def add_wgrad(d):
        zo = lax.rem(z + d, 8)
        rows = a_all[pl.ds(zo, 1)].reshape(256, 1024)
        errors = jnp.concatenate([back[zo, 0], back[zo, 1]], axis=1)
        term = jnp.dot(errors, rows, preferred_element_type=F32)
        if d == 0:
            w_acc[...] = term
        else:
            w_acc[...] += term

    for step in range(2, 5):
        for rh in range(2):
            for h in range(2):
                for s, by in sides:
                    from_ag[rh, h, s, step - 1].wait_recv()
                    zo = lax.rem(z + (-by * (step - 1)) % 8, 8)
                    at, size = h * 128, 128
                    if step == 4:
                        at, size = at + s * 64, 64
                    slot = back.at[zo, halves[rh], at : at + size]
                    from_ag[rh, h, s, step] = net.copy(slot, slot, net.peer(z=by))
        if step == 2:
            add_wgrad(0)
        add_wgrad(step - 1)
        add_wgrad(9 - step)

    for copy in small_z:
        copy.wait_recv()
    loss_g[g] = jnp.sum(loss_z[...], axis=0)
    small_g = [net.copy(loss_g.at[g], loss_g.at[g], net.peer(**o)) for o in GROUP]

    for rh in range(2):
        for h in range(2):
            for s, _ in sides:
                from_ag[rh, h, s, 4].wait_recv()
    add_wgrad(4)

    for k in range(4):
        w_send[k] = w_acc[:, k * 256 : (k + 1) * 256].reshape(8, 32, 256).astype(BF)
    from_t, from_w2 = [], []
    for offsets in PLANE:
        p = net.peer(**offsets)
        from_t.append(
            net.copy(
                w_send.at[p["xl"] * 2 + p["c"], p["xh"] * 4 + p["y"]], w_recv.at[g, t], p
            )
        )
    w_recv[g, t] = w_send[g, t]
    for copy in small_g:
        copy.wait_recv()
    loss_t[t] = jnp.sum(loss_g[...], axis=0)
    small_t = [net.copy(loss_t.at[t], loss_t.at[t], net.peer(**o)) for o in TASKS]
    for copy in from_t:
        copy.wait_recv()
    for k in range(4):
        w_all[k, t] = jnp.sum(w_recv[k].astype(F32), axis=0).astype(BF)
    mine = w_all.at[:, t]
    for offsets in TASKS:
        from_w2.append(net.copy(mine, mine, net.peer(**offsets)))
    for copy in small_t:
        copy.wait_recv()
    loss_out[...] = jnp.sum(loss_t[...], axis=0)[0:1, 0:1]
    for copy in from_w2:
        copy.wait_recv()
    stores = []
    for k in range(8):
        cut = slice(k * 128, k * 128 + 128)
        block = w_all[k // 2, 4 * (k % 2) : 4 * (k % 2) + 4].reshape(128, 256).astype(F32).T
        grad[:, cut] = (8192 * 1024) * tau[:, cut].astype(F32) * block
        store = pltpu.make_async_copy(grad.at[:, cut], out_hbm.at[:, cut], local_sem.at[8 + k])
        store.start()
        stores.append(store)
    for store in stores:
        store.wait()
    net.drain()


def local(hidden, gain, tau, coeff, counts, positions):
    vmem = pl.BlockSpec(memory_space=pltpu.VMEM)
    hbm = pl.BlockSpec(memory_space=pl.ANY)
    grad, loss = pl.pallas_call(
        kernel,
        out_shape=(
            jax.ShapeDtypeStruct((256, 1024), F32),
            jax.ShapeDtypeStruct((1, 1), F32),
        ),
        in_specs=[pl.BlockSpec(memory_space=pltpu.SMEM), hbm, vmem, hbm, hbm, vmem],
        out_specs=(hbm, vmem),
        scratch_shapes=[
            pltpu.VMEM((64, 8192), BF),
            pltpu.VMEM((256, 1024), BF),
            pltpu.VMEM((256, 1024), F32),
            pltpu.VMEM((8, 64, 1024), BF),
            pltpu.VMEM((8, 2, 2, 64, 1024), BF),
            pltpu.VMEM((4, 256, 256), BF),
            pltpu.VMEM((256, 1024), BF),
            pltpu.VMEM((4, 4, 2, 32, 256), F32),
            pltpu.VMEM((3, 4, 2, 32, 256), F32),
            pltpu.VMEM((4, 2, 32, 256), F32),
            pltpu.VMEM((2, 4, 2, 32, 256), F32),
            pltpu.VMEM((4, 2, 32, 1024), BF),
            pltpu.VMEM((8, 2, 256, 128), F32),
            pltpu.VMEM((2, 2, 2, 4, 128, 128), BF),
            pltpu.VMEM((2, 2, 2, 4, 128, 128), BF),
            pltpu.VMEM((8, 2, 256, 128), BF),
            pltpu.VMEM((256, 1024), F32),
            pltpu.VMEM((4, 8, 32, 256), BF),
            pltpu.VMEM((4, 8, 32, 256), BF),
            pltpu.VMEM((4, 8, 32, 256), BF),
            pltpu.VMEM((256, 1024), F32),
            pltpu.VMEM((2, 2, 8, 128), jnp.int32),
            pltpu.VMEM((8, 8, 128), F32),
            pltpu.VMEM((4, 8, 128), F32),
            pltpu.VMEM((8, 8, 128), F32),
            pltpu.SemaphoreType.DMA((N_SEM,)),
            pltpu.SemaphoreType.DMA((N_SEM,)),
            pltpu.SemaphoreType.DMA((16,)),
        ],
        compiler_params=pltpu.CompilerParams(
            collective_id=0, has_side_effects=True, vmem_limit_bytes=56 * 2**20
        ),
        name="step",
    )(counts, hidden[0], gain.reshape(1, -1), tau[0], coeff[0], positions)
    return grad[None], loss[0, 0]


def solution(mesh):
    spec = P("task", "mp", None)
    return jax.shard_map(
        local,
        mesh=mesh,
        in_specs=(spec, P(), spec, spec, P("task"), P("task", "mp")),
        out_specs=(spec, P()),
        check_vma=False,
    )
```

```python
import jax
import jax.numpy as jnp
from jax import lax
from jax.experimental import pallas as pl
from jax.experimental.pallas import tpu as pltpu
from jax.sharding import PartitionSpec as P

MESH = pl.DeviceIdType.MESH
BF = jnp.bfloat16
F32 = jnp.float32
HEAD = 128
SIZES = dict(xh=2, y=4, xl=2, z=8, c=2)
GROUP = (dict(c=1), dict(xl=1), dict(xl=1, c=1))
EIGHT = GROUP + tuple(dict(xh=1, **o) for o in (dict(),) + GROUP)
TASKS = tuple(dict(xh=a, y=b) for a in (1, 0) for b in (2, 1, 3, 0) if (a, b) != (0, 0))
PLANE = tuple(
    dict(xh=a, y=b, xl=k, c=d)
    for a in (1, 0)
    for b in (2, 1, 3, 0)
    for k in (1, 0)
    for d in (0, 1)
    if (a, b, k, d) != (0, 0, 0, 0)
)
RING = (1, 7, 2, 6, 3, 5, 4)
N_SEM = 192

FIRST = 4
ORDER = (
    ('q', 0),
    ('q', 1),
    ('s', 4),
    ('s', 5),
    ('f', 0),
    ('f', 1),
    ('t',),
    ('q', 2),
    ('q', 3),
    ('s', 6),
    ('y',),
    ('f', 2),
    ('f', 3),
    ('e',),
    ('p', 0),
    ('p', 1),
    ('p', 2),
    ('q', 4),
    ('f', 4),
    ('q', 5),
    ('f', 5),
    ('q', 6),
    ('f', 6),
    ('p', 3),
    ('p', 4),
)
RSORDER = ("a1", "P", "b1", "a2", "b2", "a3", "b3")


class Links:
    def __init__(self, here, send, recv):
        self.here, self.send, self.recv, self.used, self.open = here, send, recv, 0, []

    def peer(self, **offsets):
        p = dict(self.here)
        for axis, by in offsets.items():
            p[axis] = lax.rem(p[axis] + (by % SIZES[axis]), SIZES[axis])
        return p

    def device(self, p):
        return (p["xh"] * 4 + p["y"], p["xl"] * 16 + p["z"] * 2 + p["c"])

    def copy(self, src, dst, p):
        i = self.used
        self.used += 1
        made = pltpu.make_async_remote_copy(
            src_ref=src,
            dst_ref=dst,
            send_sem=self.send.at[i],
            recv_sem=self.recv.at[i],
            device_id=self.device(p),
            device_id_type=MESH,
        )
        made.start()
        self.open.append(made)
        return made

    def drain(self):
        for made in self.open:
            made.wait_send()


def nt(a, b):
    return lax.dot_general(a, b, (((1,), (1,)), ((), ())), preferred_element_type=F32)


def kernel(
    counts,
    hidden_hbm,
    gain,
    tau_hbm,
    coeff_hbm,
    pos,
    out_hbm,
    loss_out,
    hidden,
    tau,
    coeff,
    ns,
    a_all,
    tau_own,
    tau_t,
    m_own,
    m_recv,
    m_half,
    m_recv2,
    merged,
    gap,
    rs_send,
    rs_recv,
    back,
    w_acc,
    w_send,
    w_recv,
    w_all,
    grad,
    pos_all,
    loss_z,
    loss_g,
    loss_t,
    send_sem,
    recv_sem,
    local_sem,
):
    loads = [
        pltpu.make_async_copy(src, dst, local_sem.at[i])
        for i, (src, dst) in enumerate(((tau_hbm, tau), (coeff_hbm, coeff), (hidden_hbm, hidden)))
    ]
    for load in loads:
        load.start()

    t, m = lax.axis_index("task"), lax.axis_index("mp")
    me = dict(
        xh=lax.div(t, 4),
        y=lax.rem(t, 4),
        xl=lax.div(m, 16),
        z=lax.rem(lax.div(m, 2), 8),
        c=lax.rem(m, 2),
    )
    net = Links(me, send_sem, recv_sem)
    xl, z, c, y, xh = me["xl"], me["z"], me["c"], me["y"], me["xh"]
    g = xl * 2 + c

    barrier = pltpu.get_barrier_semaphore()
    partners = [dict(z=d) for d in RING] + list(PLANE)
    for offsets in partners:
        pl.semaphore_signal(
            barrier, inc=1, device_id=net.device(net.peer(**offsets)), device_id_type=MESH
        )

    loads[0].wait()
    loads[1].wait()
    for k in range(8):
        cut = slice(k * 128, (k + 1) * 128)
        tau_f = tau[:, cut].astype(F32)
        mixed_t = (coeff[:, cut] * tau_f).T
        m_own[k // 2, 2 * (k % 2) : 2 * (k % 2) + 2] = mixed_t.reshape(2, 2, 32, 256)
        tau_own[k // 2, (k % 2) * 128 : (k % 2) * 128 + 128] = tau_f.T.astype(BF)

    loads[2].wait()
    total = jnp.zeros((64, 128), F32)
    for k in range(64):
        x = hidden[:, k * 128 : (k + 1) * 128].astype(F32)
        total = total + x * x
    inverse = 1.0 / jnp.sqrt(jnp.sum(total, axis=1, keepdims=True) * (1.0 / 8192.0) + 1e-06)
    inverse = jnp.broadcast_to(inverse, (64, 128))
    for k in range(8):
        for half in range(2):
            for part in range(4):
                at = half * 4096 + k * 512 + part * 128
                x = hidden[:, at : at + 128].astype(F32)
                to = half * 512 + part * 128
                ns[k, :, to : to + 128] = (x * inverse * gain[:, at : at + 128]).astype(BF)

    pl.semaphore_wait(barrier, len(partners))

    from_y = []
    for i, d in enumerate((2, 1, 3)):
        p = net.peer(y=d)
        from_y.append(net.copy(m_own.at[:, p["y"]], m_recv.at[i], p))

    from_z = []

    def send_z(i):
        p = net.peer(z=RING[i])
        from_z.append(net.copy(ns.at[p["z"]], a_all.at[z, xl, c], p))

    for i in range(FIRST):
        send_z(i)
    sib, xn = net.peer(c=1), net.peer(xl=1)
    own_slot = a_all.at[z, xl, c]
    keep = pltpu.make_async_copy(ns.at[z], own_slot, local_sem.at[3])
    keep.start()
    to_sib, to_x, second = [], [], []
    to_sib.append(net.copy(ns.at[z], own_slot, sib))
    to_x.append(net.copy(ns.at[z], own_slot, xn))

    features = pl.ds(pl.multiple_of(g * 256, 256), 256)
    from_tau = []
    for offsets in GROUP:
        p = net.peer(**offsets)
        from_tau.append(net.copy(tau_own.at[p["xl"] * 2 + p["c"]], tau_t.at[:, features], p))
    keep_tau = pltpu.make_async_copy(tau_own.at[g], tau_t.at[:, features], local_sem.at[4])
    keep_tau.start()

    lanes = lax.broadcasted_iota(jnp.int32, (8, 128), 1)
    twice = jnp.concatenate([pos[...], pos[...]], axis=1)
    pos_all[xl, c] = jnp.where(lax.div(lanes, 64) == c, jnp.broadcast_to(twice, (8, 128)), 0)
    small = []
    for offsets in GROUP:
        small.append(net.copy(pos_all.at[xl, c], pos_all.at[xl, c], net.peer(**offsets)))

    def slot_of(i):
        return a_all.at[lax.rem(z + (8 - RING[i]), 8), xl, c]

    def arrived(i):
        from_z[i].wait_recv()
        to_sib.append(net.copy(slot_of(i), slot_of(i), sib))

    def forward(i):
        to_x.append(net.copy(slot_of(i), slot_of(i), xn))

    def pass_on(i):
        to_x[i].wait_recv()
        origin = z if i == 0 else lax.rem(z + (8 - RING[i - 1]), 8)
        slot = a_all.at[origin, 1 - xl, c]
        second.append(net.copy(slot, slot, sib))

    halves = (xl, 1 - xl)
    cosine, sine = [], []
    from_y2, from_eight = [], []

    def tables():
        for copy in small:
            copy.wait_recv()
        index = lax.broadcasted_iota(jnp.int32, (64, 128), 0).astype(F32)
        freq = jnp.exp(-jnp.log(F32(1000000.0)) * 2.0 * index / HEAD)
        for xr in halves:
            at_rows = pos_all[xr, 0] + pos_all[xr, 1]
            angle = at_rows[0:1].astype(F32) * freq
            cosine.append(jnp.cos(angle))
            sine.append(jnp.sin(angle))

    def sum_y():
        for copy in from_y:
            copy.wait_recv()
        m_half[...] = (
            m_own[:, pl.ds(y, 1)].reshape(4, 2, 32, 256) + m_recv[0] + m_recv[1] + m_recv[2]
        )
        m_recv2[xh, g] = m_half[g]
        for offsets in EIGHT:
            p = net.peer(**offsets)
            from_eight.append(net.copy(m_half.at[p["xl"] * 2 + p["c"]], m_recv2.at[xh, g], p))

    def spread_y():
        for copy in from_eight:
            copy.wait_recv()
        for k in range(4):
            merged[y, :, :, k * 256 : (k + 1) * 256] = (m_recv2[0, k] + m_recv2[1, k]).astype(BF)
        for d in (2, 1, 3):
            from_y2.append(net.copy(merged.at[y], merged.at[y], net.peer(y=d)))

    for what, *i in ORDER:
        dict(f=forward, q=arrived, p=pass_on, t=tables, y=sum_y, e=spread_y, s=send_z)[what](*i)

    keep.wait()
    keep_tau.wait()
    for copy in from_tau + to_sib + from_y2:
        copy.wait_recv()

    def partial_gap(d, rh):
        zd = lax.rem(z + d, 8)
        rows = a_all[pl.ds(zd, 1), pl.ds(halves[rh], 1)].reshape(128, 1024)
        gap[zd, rh] = nt(merged[...].reshape(256, 1024), rows) - nt(tau_t[...], rows)

    sides = ((0, 1), (1, 7))
    from_rs = {}

    def rs_send_to(rh, h, s, slot, by, rows=slice(0, 128)):
        from_rs[rh, h, s, slot] = net.copy(
            rs_send.at[rh, h, s, slot, rows], rs_recv.at[rh, h, s, slot, rows], net.peer(z=by)
        )

    def terms_of(rh, h, d):
        return gap[lax.rem(z + d % 8, 8), rh, h * 128 : h * 128 + 128]

    def rs_step(step, rh):
        if step == 1:
            partial_gap(4, rh)
            for h in range(2):
                for s, by in sides:
                    half = slice(s * 64, s * 64 + 64)
                    rs_send[rh, h, s, 0, half] = terms_of(rh, h, 4)[half].astype(BF)
                    rs_send_to(rh, h, s, 0, 2 * by, half)
            for s, by in sides:
                partial_gap(3 * by % 8, rh)
                for h in range(2):
                    rs_send[rh, h, s, 1] = terms_of(rh, h, 3 * by).astype(BF)
                    rs_send_to(rh, h, s, 1, by)
            return
        d = 4 - step
        partial_gap(d, rh)
        partial_gap(8 - d, rh)
        for h in range(2):
            for s, by in sides:
                from_rs[rh, h, s, step - 1].wait_recv()
                terms = terms_of(rh, h, d * by) + rs_recv[rh, h, s, step - 1].astype(F32)
                if step == 2:
                    half = slice(s * 64, s * 64 + 64)
                    other = slice(64 - s * 64, 128 - s * 64)
                    from_rs[rh, h, s, 0].wait_recv()
                    rs_send[rh, h, s, 2, half] = (
                        terms[half] + rs_recv[rh, h, s, 0, half].astype(F32)
                    ).astype(BF)
                    rs_send[rh, h, s, 2, other] = terms[other].astype(BF)
                else:
                    rs_send[rh, h, s, 3] = terms.astype(BF)
                rs_send_to(rh, h, s, step, by)

    for what in RSORDER:
        if what == "P":
            for i in range(len(second), 8):
                pass_on(i)
            for copy in second:
                copy.wait_recv()
        else:
            rs_step(int(what[1]), "ab".index(what[0]))
    partial_gap(0, 0)
    partial_gap(0, 1)

    squares = jnp.zeros((64, 128), F32)
    lane = lax.broadcasted_iota(jnp.int32, (1, 128), 1)
    count = jnp.full((1, 128), counts[0], jnp.int32)
    scale = 1.0 / (count.astype(F32) * 1024.0)
    from_ag = {}
    for rh in range(2):
        row = halves[rh] * 1024 + z * 128 + lane
        live = (row < count).astype(F32)
        weight = 2.0 * scale * live
        for h in range(2):
            for s, _ in sides:
                from_rs[rh, h, s, 3].wait_recv()
            at = h * 128
            full = (
                gap[z, rh, at : at + 128]
                + rs_recv[rh, h, 0, 3].astype(F32)
                + rs_recv[rh, h, 1, 3].astype(F32)
            )
            first, last = full[0:64], full[64:128]
            err_a = first * cosine[rh] - last * sine[rh]
            err_b = last * cosine[rh] + first * sine[rh]
            squares = squares + (live * err_a * err_a + live * err_b * err_b) * scale
            err_a, err_b = weight * err_a, weight * err_b
            slot = back.at[z, halves[rh], at : at + 128]
            slot[0:64] = (err_a * cosine[rh] + err_b * sine[rh]).astype(BF)
            slot[64:128] = (err_b * cosine[rh] - err_a * sine[rh]).astype(BF)
            for s, by in sides:
                from_ag[rh, h, s, 1] = net.copy(slot, slot, net.peer(z=by))

    def tile_of(value):
        return jnp.broadcast_to(value, (8, 128))

    loss_z[z] = tile_of(jnp.sum(squares, keepdims=True))
    small_z = [net.copy(loss_z.at[z], loss_z.at[z], net.peer(z=d)) for d in RING]

    def add_wgrad(d):
        zo = lax.rem(z + d, 8)
        rows = a_all[pl.ds(zo, 1)].reshape(256, 1024)
        errors = jnp.concatenate([back[zo, 0], back[zo, 1]], axis=1)
        term = jnp.dot(errors, rows, preferred_element_type=F32)
        if d == 0:
            w_acc[...] = term
        else:
            w_acc[...] += term

    for step in range(2, 5):
        for rh in range(2):
            for h in range(2):
                for s, by in sides:
                    from_ag[rh, h, s, step - 1].wait_recv()
                    zo = lax.rem(z + (-by * (step - 1)) % 8, 8)
                    at, size = h * 128, 128
                    if step == 4:
                        at, size = at + s * 64, 64
                    slot = back.at[zo, halves[rh], at : at + size]
                    from_ag[rh, h, s, step] = net.copy(slot, slot, net.peer(z=by))
        if step == 2:
            add_wgrad(0)
        add_wgrad(step - 1)
        add_wgrad(9 - step)

    for copy in small_z:
        copy.wait_recv()
    loss_g[g] = jnp.sum(loss_z[...], axis=0)
    small_g = [net.copy(loss_g.at[g], loss_g.at[g], net.peer(**o)) for o in GROUP]

    for rh in range(2):
        for h in range(2):
            for s, _ in sides:
                from_ag[rh, h, s, 4].wait_recv()
    add_wgrad(4)

    for k in range(4):
        w_send[k] = w_acc[:, k * 256 : (k + 1) * 256].reshape(8, 32, 256).astype(BF)
    from_t, from_w2 = [], []
    for offsets in PLANE:
        p = net.peer(**offsets)
        from_t.append(
            net.copy(
                w_send.at[p["xl"] * 2 + p["c"], p["xh"] * 4 + p["y"]], w_recv.at[g, t], p
            )
        )
    w_recv[g, t] = w_send[g, t]
    for copy in small_g:
        copy.wait_recv()
    loss_t[t] = jnp.sum(loss_g[...], axis=0)
    small_t = [net.copy(loss_t.at[t], loss_t.at[t], net.peer(**o)) for o in TASKS]
    for copy in from_t:
        copy.wait_recv()
    for k in range(4):
        w_all[k, t] = jnp.sum(w_recv[k].astype(F32), axis=0).astype(BF)
    mine = w_all.at[:, t]
    for offsets in TASKS:
        from_w2.append(net.copy(mine, mine, net.peer(**offsets)))
    for copy in small_t:
        copy.wait_recv()
    loss_out[...] = jnp.sum(loss_t[...], axis=0)[0:1, 0:1]
    for copy in from_w2:
        copy.wait_recv()
    stores = []
    for k in range(8):
        cut = slice(k * 128, k * 128 + 128)
        block = w_all[k // 2, 4 * (k % 2) : 4 * (k % 2) + 4].reshape(128, 256).astype(F32).T
        grad[:, cut] = (8192 * 1024) * tau[:, cut].astype(F32) * block
        store = pltpu.make_async_copy(grad.at[:, cut], out_hbm.at[:, cut], local_sem.at[8 + k])
        store.start()
        stores.append(store)
    for store in stores:
        store.wait()
    net.drain()


def local(hidden, gain, tau, coeff, counts, positions):
    vmem = pl.BlockSpec(memory_space=pltpu.VMEM)
    hbm = pl.BlockSpec(memory_space=pl.ANY)
    grad, loss = pl.pallas_call(
        kernel,
        out_shape=(
            jax.ShapeDtypeStruct((256, 1024), F32),
            jax.ShapeDtypeStruct((1, 1), F32),
        ),
        in_specs=[pl.BlockSpec(memory_space=pltpu.SMEM), hbm, vmem, hbm, hbm, vmem],
        out_specs=(hbm, vmem),
        scratch_shapes=[
            pltpu.VMEM((64, 8192), BF),
            pltpu.VMEM((256, 1024), BF),
            pltpu.VMEM((256, 1024), F32),
            pltpu.VMEM((8, 64, 1024), BF),
            pltpu.VMEM((8, 2, 2, 64, 1024), BF),
            pltpu.VMEM((4, 256, 256), BF),
            pltpu.VMEM((256, 1024), BF),
            pltpu.VMEM((4, 4, 2, 32, 256), F32),
            pltpu.VMEM((3, 4, 2, 32, 256), F32),
            pltpu.VMEM((4, 2, 32, 256), F32),
            pltpu.VMEM((2, 4, 2, 32, 256), F32),
            pltpu.VMEM((4, 2, 32, 1024), BF),
            pltpu.VMEM((8, 2, 256, 128), F32),
            pltpu.VMEM((2, 2, 2, 4, 128, 128), BF),
            pltpu.VMEM((2, 2, 2, 4, 128, 128), BF),
            pltpu.VMEM((8, 2, 256, 128), BF),
            pltpu.VMEM((256, 1024), F32),
            pltpu.VMEM((4, 8, 32, 256), BF),
            pltpu.VMEM((4, 8, 32, 256), BF),
            pltpu.VMEM((4, 8, 32, 256), BF),
            pltpu.VMEM((256, 1024), F32),
            pltpu.VMEM((2, 2, 8, 128), jnp.int32),
            pltpu.VMEM((8, 8, 128), F32),
            pltpu.VMEM((4, 8, 128), F32),
            pltpu.VMEM((8, 8, 128), F32),
            pltpu.SemaphoreType.DMA((N_SEM,)),
            pltpu.SemaphoreType.DMA((N_SEM,)),
            pltpu.SemaphoreType.DMA((16,)),
        ],
        compiler_params=pltpu.CompilerParams(
            collective_id=0, has_side_effects=True, vmem_limit_bytes=56 * 2**20
        ),
        name="step",
    )(counts, hidden[0], gain.reshape(1, -1), tau[0], coeff[0], positions)
    return grad[None], loss[0, 0]


def solution(mesh):
    spec = P("task", "mp", None)
    return jax.shard_map(
        local,
        mesh=mesh,
        in_specs=(spec, P(), spec, spec, P("task"), P("task", "mp")),
        out_specs=(spec, P()),
        check_vma=False,
    )
```

```python
import jax
import jax.numpy as jnp
from jax import lax
from jax.experimental import pallas as pl
from jax.experimental.pallas import tpu as pltpu
from jax.sharding import PartitionSpec as P

MESH = pl.DeviceIdType.MESH
BF = jnp.bfloat16
F32 = jnp.float32
HEAD = 128
SIZES = dict(xh=2, y=4, xl=2, z=8, c=2)
GROUP = (dict(c=1), dict(xl=1), dict(xl=1, c=1))
EIGHT = GROUP + tuple(dict(xh=1, **o) for o in (dict(),) + GROUP)
TASKS = tuple(dict(xh=a, y=b) for a in (1, 0) for b in (2, 1, 3, 0) if (a, b) != (0, 0))
PLANE = tuple(
    dict(xh=a, y=b, xl=k, c=d)
    for a in (1, 0)
    for b in (2, 1, 3, 0)
    for k in (1, 0)
    for d in (0, 1)
    if (a, b, k, d) != (0, 0, 0, 0)
)
RING = (1, 7, 2, 6, 3, 5, 4)
N_SEM = 192

FIRST = 4
ORDER = (
    ('q', 0),
    ('q', 1),
    ('s', 4),
    ('s', 5),
    ('f', 0),
    ('f', 1),
    ('t',),
    ('q', 2),
    ('q', 3),
    ('s', 6),
    ('y',),
    ('f', 2),
    ('f', 3),
    ('e',),
    ('p', 0),
    ('p', 1),
    ('p', 2),
    ('q', 4),
    ('f', 4),
    ('q', 5),
    ('f', 5),
    ('q', 6),
    ('f', 6),
    ('p', 3),
    ('p', 4),
)
RSORDER = ("a1", "P", "b1", "a2", "b2", "a3", "b3")


class Links:
    def __init__(self, here, send, recv):
        self.here, self.send, self.recv, self.used, self.open = here, send, recv, 0, []

    def peer(self, **offsets):
        p = dict(self.here)
        for axis, by in offsets.items():
            p[axis] = lax.rem(p[axis] + (by % SIZES[axis]), SIZES[axis])
        return p

    def device(self, p):
        return (p["xh"] * 4 + p["y"], p["xl"] * 16 + p["z"] * 2 + p["c"])

    def copy(self, src, dst, p):
        i = self.used
        self.used += 1
        made = pltpu.make_async_remote_copy(
            src_ref=src,
            dst_ref=dst,
            send_sem=self.send.at[i],
            recv_sem=self.recv.at[i],
            device_id=self.device(p),
            device_id_type=MESH,
        )
        made.start()
        self.open.append(made)
        return made

    def drain(self):
        for made in self.open:
            made.wait_send()


def nt(a, b):
    return lax.dot_general(a, b, (((1,), (1,)), ((), ())), preferred_element_type=F32)


def kernel(
    counts,
    hidden_hbm,
    gain,
    tau_hbm,
    coeff_hbm,
    pos,
    out_hbm,
    loss_out,
    hidden,
    tau,
    coeff,
    ns,
    a_all,
    tau_own,
    tau_t,
    m_own,
    m_recv,
    m_half,
    m_recv2,
    merged,
    gap,
    rs_send,
    rs_recv,
    back,
    w_acc,
    w_send,
    w_recv,
    w_all,
    grad,
    pos_all,
    loss_z,
    loss_g,
    loss_t,
    send_sem,
    recv_sem,
    local_sem,
):
    loads = [
        pltpu.make_async_copy(src, dst, local_sem.at[i])
        for i, (src, dst) in enumerate(((tau_hbm, tau), (coeff_hbm, coeff), (hidden_hbm, hidden)))
    ]
    for load in loads:
        load.start()

    t, m = lax.axis_index("task"), lax.axis_index("mp")
    me = dict(
        xh=lax.div(t, 4),
        y=lax.rem(t, 4),
        xl=lax.div(m, 16),
        z=lax.rem(lax.div(m, 2), 8),
        c=lax.rem(m, 2),
    )
    net = Links(me, send_sem, recv_sem)
    xl, z, c, y, xh = me["xl"], me["z"], me["c"], me["y"], me["xh"]
    g = xl * 2 + c

    barrier = pltpu.get_barrier_semaphore()
    partners = [dict(z=d) for d in RING] + list(PLANE)
    for offsets in partners:
        pl.semaphore_signal(
            barrier, inc=1, device_id=net.device(net.peer(**offsets)), device_id_type=MESH
        )

    loads[0].wait()
    loads[1].wait()
    for k in range(8):
        cut = slice(k * 128, (k + 1) * 128)
        tau_f = tau[:, cut].astype(F32)
        mixed_t = (coeff[:, cut] * tau_f).T
        m_own[k // 2, 2 * (k % 2) : 2 * (k % 2) + 2] = mixed_t.reshape(2, 2, 32, 256)
        tau_own[k // 2, (k % 2) * 128 : (k % 2) * 128 + 128] = tau_f.T.astype(BF)

    loads[2].wait()
    total = jnp.zeros((64, 128), F32)
    for k in range(64):
        x = hidden[:, k * 128 : (k + 1) * 128].astype(F32)
        total = total + x * x
    inverse = 1.0 / jnp.sqrt(jnp.sum(total, axis=1, keepdims=True) * (1.0 / 8192.0) + 1e-06)
    inverse = jnp.broadcast_to(inverse, (64, 128))
    for k in range(8):
        for half in range(2):
            for part in range(4):
                at = half * 4096 + k * 512 + part * 128
                x = hidden[:, at : at + 128].astype(F32)
                to = half * 512 + part * 128
                ns[k, :, to : to + 128] = (x * inverse * gain[:, at : at + 128]).astype(BF)

    pl.semaphore_wait(barrier, len(partners))

    from_y = []
    for i, d in enumerate((2, 1, 3)):
        p = net.peer(y=d)
        from_y.append(net.copy(m_own.at[:, p["y"]], m_recv.at[i], p))

    from_z = []

    def send_z(i):
        p = net.peer(z=RING[i])
        from_z.append(net.copy(ns.at[p["z"]], a_all.at[z, xl, c], p))

    for i in range(FIRST):
        send_z(i)
    sib, xn = net.peer(c=1), net.peer(xl=1)
    own_slot = a_all.at[z, xl, c]
    keep = pltpu.make_async_copy(ns.at[z], own_slot, local_sem.at[3])
    keep.start()
    to_sib, to_x, second = [], [], []
    to_sib.append(net.copy(ns.at[z], own_slot, sib))
    to_x.append(net.copy(ns.at[z], own_slot, xn))

    features = pl.ds(pl.multiple_of(g * 256, 256), 256)
    from_tau = []
    for offsets in GROUP:
        p = net.peer(**offsets)
        from_tau.append(net.copy(tau_own.at[p["xl"] * 2 + p["c"]], tau_t.at[:, features], p))
    keep_tau = pltpu.make_async_copy(tau_own.at[g], tau_t.at[:, features], local_sem.at[4])
    keep_tau.start()

    lanes = lax.broadcasted_iota(jnp.int32, (8, 128), 1)
    twice = jnp.concatenate([pos[...], pos[...]], axis=1)
    pos_all[xl, c] = jnp.where(lax.div(lanes, 64) == c, jnp.broadcast_to(twice, (8, 128)), 0)
    small = []
    for offsets in GROUP:
        small.append(net.copy(pos_all.at[xl, c], pos_all.at[xl, c], net.peer(**offsets)))

    def slot_of(i):
        return a_all.at[lax.rem(z + (8 - RING[i]), 8), xl, c]

    def arrived(i):
        from_z[i].wait_recv()
        to_sib.append(net.copy(slot_of(i), slot_of(i), sib))

    def forward(i):
        to_x.append(net.copy(slot_of(i), slot_of(i), xn))

    def pass_on(i):
        to_x[i].wait_recv()
        origin = z if i == 0 else lax.rem(z + (8 - RING[i - 1]), 8)
        slot = a_all.at[origin, 1 - xl, c]
        second.append(net.copy(slot, slot, sib))

    halves = (xl, 1 - xl)
    cosine, sine = [], []
    from_y2, from_eight = [], []

    def tables():
        for copy in small:
            copy.wait_recv()
        index = lax.broadcasted_iota(jnp.int32, (64, 128), 0).astype(F32)
        freq = jnp.exp(-jnp.log(F32(1000000.0)) * 2.0 * index / HEAD)
        for xr in halves:
            at_rows = pos_all[xr, 0] + pos_all[xr, 1]
            angle = at_rows[0:1].astype(F32) * freq
            cosine.append(jnp.cos(angle))
            sine.append(jnp.sin(angle))

    def sum_y():
        for copy in from_y:
            copy.wait_recv()
        m_half[...] = (
            m_own[:, pl.ds(y, 1)].reshape(4, 2, 32, 256) + m_recv[0] + m_recv[1] + m_recv[2]
        )
        m_recv2[xh, g] = m_half[g]
        for offsets in EIGHT:
            p = net.peer(**offsets)
            from_eight.append(net.copy(m_half.at[p["xl"] * 2 + p["c"]], m_recv2.at[xh, g], p))

    def spread_y():
        for copy in from_eight:
            copy.wait_recv()
        for k in range(4):
            merged[y, :, :, k * 256 : (k + 1) * 256] = (m_recv2[0, k] + m_recv2[1, k]).astype(BF)
        for d in (2, 1, 3):
            from_y2.append(net.copy(merged.at[y], merged.at[y], net.peer(y=d)))

    for what, *i in ORDER:
        dict(f=forward, q=arrived, p=pass_on, t=tables, y=sum_y, e=spread_y, s=send_z)[what](*i)

    keep.wait()
    keep_tau.wait()
    for copy in from_tau + to_sib + from_y2:
        copy.wait_recv()

    def partial_gap(d, rh):
        zd = lax.rem(z + d, 8)
        rows = a_all[pl.ds(zd, 1), pl.ds(halves[rh], 1)].reshape(128, 1024)
        gap[zd, rh] = nt(merged[...].reshape(256, 1024), rows) - nt(tau_t[...], rows)

    sides = ((0, 1), (1, 7))
    from_rs = {}

    def rs_send_to(rh, h, s, slot, by, rows=slice(0, 128)):
        from_rs[rh, h, s, slot] = net.copy(
            rs_send.at[rh, h, s, slot, rows], rs_recv.at[rh, h, s, slot, rows], net.peer(z=by)
        )

    def terms_of(rh, h, d):
        return gap[lax.rem(z + d % 8, 8), rh, h * 128 : h * 128 + 128]

    def rs_step(step, rh):
        if step == 1:
            partial_gap(4, rh)
            for h in range(2):
                for s, by in sides:
                    half = slice(s * 64, s * 64 + 64)
                    rs_send[rh, h, s, 0, half] = terms_of(rh, h, 4)[half].astype(BF)
                    rs_send_to(rh, h, s, 0, 2 * by, half)
            for s, by in sides:
                partial_gap(3 * by % 8, rh)
                for h in range(2):
                    rs_send[rh, h, s, 1] = terms_of(rh, h, 3 * by).astype(BF)
                    rs_send_to(rh, h, s, 1, by)
            return
        d = 4 - step
        partial_gap(d, rh)
        partial_gap(8 - d, rh)
        for h in range(2):
            for s, by in sides:
                from_rs[rh, h, s, step - 1].wait_recv()
                terms = terms_of(rh, h, d * by) + rs_recv[rh, h, s, step - 1].astype(F32)
                if step == 2:
                    half = slice(s * 64, s * 64 + 64)
                    other = slice(64 - s * 64, 128 - s * 64)
                    from_rs[rh, h, s, 0].wait_recv()
                    rs_send[rh, h, s, 2, half] = (
                        terms[half] + rs_recv[rh, h, s, 0, half].astype(F32)
                    ).astype(BF)
                    rs_send[rh, h, s, 2, other] = terms[other].astype(BF)
                else:
                    rs_send[rh, h, s, 3] = terms.astype(BF)
                rs_send_to(rh, h, s, step, by)

    for what in RSORDER:
        if what == "P":
            for i in range(len(second), 8):
                pass_on(i)
            for copy in second:
                copy.wait_recv()
        else:
            rs_step(int(what[1]), "ab".index(what[0]))
    partial_gap(0, 0)
    partial_gap(0, 1)

    squares = jnp.zeros((64, 128), F32)
    lane = lax.broadcasted_iota(jnp.int32, (1, 128), 1)
    count = jnp.full((1, 128), counts[0], jnp.int32)
    scale = 1.0 / (count.astype(F32) * 1024.0)
    from_ag = {}
    for rh in range(2):
        row = halves[rh] * 1024 + z * 128 + lane
        live = (row < count).astype(F32)
        weight = 2.0 * scale * live
        for h in range(2):
            for s, _ in sides:
                from_rs[rh, h, s, 3].wait_recv()
            at = h * 128
            full = (
                gap[z, rh, at : at + 128]
                + rs_recv[rh, h, 0, 3].astype(F32)
                + rs_recv[rh, h, 1, 3].astype(F32)
            )
            first, last = full[0:64], full[64:128]
            err_a = first * cosine[rh] - last * sine[rh]
            err_b = last * cosine[rh] + first * sine[rh]
            squares = squares + (live * err_a * err_a + live * err_b * err_b) * scale
            err_a, err_b = weight * err_a, weight * err_b
            slot = back.at[z, halves[rh], at : at + 128]
            slot[0:64] = (err_a * cosine[rh] + err_b * sine[rh]).astype(BF)
            slot[64:128] = (err_b * cosine[rh] - err_a * sine[rh]).astype(BF)
            for s, by in sides:
                from_ag[rh, h, s, 1] = net.copy(slot, slot, net.peer(z=by))

    def tile_of(value):
        return jnp.broadcast_to(value, (8, 128))

    loss_z[z] = tile_of(jnp.sum(squares, keepdims=True))
    small_z = [net.copy(loss_z.at[z], loss_z.at[z], net.peer(z=d)) for d in RING]

    def add_wgrad(d):
        zo = lax.rem(z + d, 8)
        rows = a_all[pl.ds(zo, 1)].reshape(256, 1024)
        errors = jnp.concatenate([back[zo, 0], back[zo, 1]], axis=1)
        term = jnp.dot(errors, rows, preferred_element_type=F32)
        if d == 0:
            w_acc[...] = term
        else:
            w_acc[...] += term

    add_wgrad(0)
    for step in range(2, 5):
        for rh in range(2):
            for h in range(2):
                for s, by in sides:
                    from_ag[rh, h, s, step - 1].wait_recv()
                    zo = lax.rem(z + (-by * (step - 1)) % 8, 8)
                    at, size = h * 128, 128
                    if step == 4:
                        at, size = at + s * 64, 64
                    slot = back.at[zo, halves[rh], at : at + size]
                    from_ag[rh, h, s, step] = net.copy(slot, slot, net.peer(z=by))
        add_wgrad(step - 1)
        add_wgrad(9 - step)

    for copy in small_z:
        copy.wait_recv()
    loss_g[g] = jnp.sum(loss_z[...], axis=0)
    small_g = [net.copy(loss_g.at[g], loss_g.at[g], net.peer(**o)) for o in GROUP]

    for rh in range(2):
        for h in range(2):
            for s, _ in sides:
                from_ag[rh, h, s, 4].wait_recv()
    add_wgrad(4)

    for k in range(4):
        w_send[k] = w_acc[:, k * 256 : (k + 1) * 256].reshape(8, 32, 256).astype(BF)
    from_t, from_w2 = [], []
    for offsets in PLANE:
        p = net.peer(**offsets)
        from_t.append(
            net.copy(
                w_send.at[p["xl"] * 2 + p["c"], p["xh"] * 4 + p["y"]], w_recv.at[g, t], p
            )
        )
    w_recv[g, t] = w_send[g, t]
    for copy in small_g:
        copy.wait_recv()
    loss_t[t] = jnp.sum(loss_g[...], axis=0)
    small_t = [net.copy(loss_t.at[t], loss_t.at[t], net.peer(**o)) for o in TASKS]
    for copy in from_t:
        copy.wait_recv()
    for k in range(4):
        w_all[k, t] = jnp.sum(w_recv[k].astype(F32), axis=0).astype(BF)
    mine = w_all.at[:, t]
    for offsets in TASKS:
        from_w2.append(net.copy(mine, mine, net.peer(**offsets)))
    for copy in small_t:
        copy.wait_recv()
    loss_out[...] = jnp.sum(loss_t[...], axis=0)[0:1, 0:1]
    for copy in from_w2:
        copy.wait_recv()
    stores = []
    for k in range(8):
        cut = slice(k * 128, k * 128 + 128)
        block = w_all[k // 2, 4 * (k % 2) : 4 * (k % 2) + 4].reshape(128, 256).astype(F32).T
        grad[:, cut] = (8192 * 1024) * tau[:, cut].astype(F32) * block
        store = pltpu.make_async_copy(grad.at[:, cut], out_hbm.at[:, cut], local_sem.at[8 + k])
        store.start()
        stores.append(store)
    for store in stores:
        store.wait()
    net.drain()


def local(hidden, gain, tau, coeff, counts, positions):
    vmem = pl.BlockSpec(memory_space=pltpu.VMEM)
    hbm = pl.BlockSpec(memory_space=pl.ANY)
    grad, loss = pl.pallas_call(
        kernel,
        out_shape=(
            jax.ShapeDtypeStruct((256, 1024), F32),
            jax.ShapeDtypeStruct((1, 1), F32),
        ),
        in_specs=[pl.BlockSpec(memory_space=pltpu.SMEM), hbm, vmem, hbm, hbm, vmem],
        out_specs=(hbm, vmem),
        scratch_shapes=[
            pltpu.VMEM((64, 8192), BF),
            pltpu.VMEM((256, 1024), BF),
            pltpu.VMEM((256, 1024), F32),
            pltpu.VMEM((8, 64, 1024), BF),
            pltpu.VMEM((8, 2, 2, 64, 1024), BF),
            pltpu.VMEM((4, 256, 256), BF),
            pltpu.VMEM((256, 1024), BF),
            pltpu.VMEM((4, 4, 2, 32, 256), F32),
            pltpu.VMEM((3, 4, 2, 32, 256), F32),
            pltpu.VMEM((4, 2, 32, 256), F32),
            pltpu.VMEM((2, 4, 2, 32, 256), F32),
            pltpu.VMEM((4, 2, 32, 1024), BF),
            pltpu.VMEM((8, 2, 256, 128), F32),
            pltpu.VMEM((2, 2, 2, 4, 128, 128), BF),
            pltpu.VMEM((2, 2, 2, 4, 128, 128), BF),
            pltpu.VMEM((8, 2, 256, 128), BF),
            pltpu.VMEM((256, 1024), F32),
            pltpu.VMEM((4, 8, 32, 256), BF),
            pltpu.VMEM((4, 8, 32, 256), BF),
            pltpu.VMEM((4, 8, 32, 256), BF),
            pltpu.VMEM((256, 1024), F32),
            pltpu.VMEM((2, 2, 8, 128), jnp.int32),
            pltpu.VMEM((8, 8, 128), F32),
            pltpu.VMEM((4, 8, 128), F32),
            pltpu.VMEM((8, 8, 128), F32),
            pltpu.SemaphoreType.DMA((N_SEM,)),
            pltpu.SemaphoreType.DMA((N_SEM,)),
            pltpu.SemaphoreType.DMA((16,)),
        ],
        compiler_params=pltpu.CompilerParams(
            collective_id=0, has_side_effects=True, vmem_limit_bytes=56 * 2**20
        ),
        name="step",
    )(counts, hidden[0], gain.reshape(1, -1), tau[0], coeff[0], positions)
    return grad[None], loss[0, 0]


def solution(mesh):
    spec = P("task", "mp", None)
    return jax.shard_map(
        local,
        mesh=mesh,
        in_specs=(spec, P(), spec, spec, P("task"), P("task", "mp")),
        out_specs=(spec, P()),
        check_vma=False,
    )
```
